32 devices in a mesh: gx: 4 (over y, x), gy: 8 (over z, core).
Axes of the slice: x: 2, y: 2, z: 4, core: 2. Of those that a mesh axis runs over, the one named last changes fastest.
Arguments:
- old_state: float32 [8, 8, 128, 1024], P(None, None, 'gx', 'gy'), may hold values from -6 to 6
- section_prims: float32 [8, 8, 128, 1024], P(None, None, 'gx', 'gy'), may hold values from -3 to 3, as said below
- shear_whole: int32 [1], replicated, may hold values from 0 to 1023
- shear_frac: float32 [1], replicated, may hold values from 0 to 1
Outputs:
- new_state: float32 [8, 8, 128, 1024], P(None, None, 'gx', 'gy')
The draws below stay inside these ranges and needn't reach their ends.
Inputs may be any that keep to these rules, and one draw needn't show every extreme that they name: section_prims holds density in [0.5, 2] in field 0 and pressure in [0.3, 3] in field 4; the other fields lie in the stated range.
All inputs are finite; a program needn't handle non-finite values.
Results may differ from the reference program's by a relative error of at most 0.0003.
Values sent between devices are 32-bit elements; how exact they have to be, the bound alone decides.
No kernel may reach another device: no remote copies, remote signals or barrier semaphores. Data moves between devices by JAX's collectives and lax.ppermute only.
A program may use at most 128 MiB of HBM per device.

```python
import math
import jax
import jax.numpy as jnp
from jax import lax

CX = 32
NZ = 8
NF = 8
NX = 128
NY = 1024
N_GX = 4


def draw_section_prims(key, part):
    keys = jax.random.split(key, 4)
    shape = (NZ, NX, NY)
    rho = jnp.exp(jax.random.uniform(keys[0], shape, jnp.float32, math.log(0.5), math.log(2.0)))
    pres = jnp.exp(jax.random.uniform(keys[1], shape, jnp.float32, math.log(0.3), math.log(3.0)))
    vel = 0.5 * jnp.clip(jax.random.normal(keys[2], (3,) + shape, jnp.float32), -6.0, 6.0)
    mag = 0.5 * jnp.clip(jax.random.normal(keys[3], (3,) + shape, jnp.float32), -6.0, 6.0)
    return jnp.concatenate([rho[None], vel, pres[None], mag], axis=0)


def levels(key, shape, pieces, smallest, top_value):
    loudness = 1.0
    for dim, blocks in pieces:
        steps = jax.random.uniform(jax.random.fold_in(jax.random.fold_in(key, 6), dim), (blocks,), jnp.float32, smallest / len(pieces), top_value / len(pieces))
        loudness = loudness * jnp.repeat(jnp.exp(steps), shape[dim] // blocks).reshape((-1,) + (1,) * (len(shape) - 1 - dim))
    return loudness


def normal_values(own_key, extent, spread, bound, shards=(), kind=jnp.bfloat16):
    array = spread * jax.random.normal(own_key, extent, jnp.float32)
    if shards:
        array = array * levels(own_key, extent, shards, -0.22, 0.18)
    return jnp.clip(array, -bound, bound).astype(kind)


def setup_inputs(seed: int = 0) -> dict:
    streams_of = jax.random.split(jax.random.key(seed), 5)
    return {
        "old_state": normal_values(streams_of[0], (NF, NZ, NX, NY), 1.0, 6.0, ((2, 4), (3, 8)), jnp.float32),
        "section_prims": draw_section_prims(jax.random.fold_in(streams_of[4], 71), 0),
        "shear_whole": jax.random.randint(streams_of[2], (1,), 0, NY).astype(jnp.int32),
        "shear_frac": jnp.clip(jax.random.uniform(streams_of[3], (1,), jnp.float32, 0.0, 1.0), 0.0, 1.0),
    }


gamma_gas = 5.0 / 3.0
omega_rate = 1.0
shear_rate = 1.5
time_step = 0.1

def conserved(prims):
    rho = prims[0]
    kinetic = 0.5 * rho * (prims[1] * prims[1] + prims[2] * prims[2] + prims[3] * prims[3])
    magnetic = 0.5 * (prims[5] * prims[5] + prims[6] * prims[6] + prims[7] * prims[7])
    energy = prims[4] / (gamma_gas - 1.0) + kinetic + magnetic
    return jnp.stack([rho, rho * prims[1], rho * prims[2], rho * prims[3], energy, prims[5], prims[6], prims[7]])

def fluxes(prims, cons, direction):
    rho = prims[0]
    normal_vel = prims[1 + direction]
    normal_mag = prims[5 + direction]
    ptotal = prims[4] + 0.5 * (prims[5] * prims[5] + prims[6] * prims[6] + prims[7] * prims[7])
    vdotb = prims[1] * prims[5] + prims[2] * prims[6] + prims[3] * prims[7]
    parts = [rho * normal_vel]
    for comp in range(3):
        parts.append(rho * prims[1 + comp] * normal_vel - prims[5 + comp] * normal_mag)
    parts[1 + direction] = parts[1 + direction] + ptotal
    parts.append((cons[4] + ptotal) * normal_vel - normal_mag * vdotb)
    for comp in range(3):
        parts.append(prims[5 + comp] * normal_vel - prims[1 + comp] * normal_mag)
    return jnp.stack(parts)

def fast_speed(prims, direction):
    rho = prims[0]
    sound = gamma_gas * prims[4] / rho
    squares = [prims[5] * prims[5], prims[6] * prims[6], prims[7] * prims[7]]
    alfven = (squares[0] + squares[1] + squares[2]) / rho
    others = [squares[c] for c in range(3) if c != direction]
    transverse = (others[0] + others[1]) / rho
    disc = jnp.square(sound - alfven) + 4.0 * sound * transverse
    return jnp.sqrt(0.5 * (sound + alfven + jnp.sqrt(disc)))

def minmod(first, second):
    return 0.5 * (jnp.sign(first) + jnp.sign(second)) * jnp.minimum(jnp.abs(first), jnp.abs(second))

def rusanov(left, right, direction):
    cons_left = conserved(left)
    cons_right = conserved(right)
    flux_left = fluxes(left, cons_left, direction)
    flux_right = fluxes(right, cons_right, direction)
    speed_left = jnp.abs(left[1 + direction]) + fast_speed(left, direction)
    speed_right = jnp.abs(right[1 + direction]) + fast_speed(right, direction)
    speed = jnp.maximum(speed_left, speed_right)
    return 0.5 * (flux_left + flux_right) - 0.5 * speed * (cons_right - cons_left)

def sweep(padded, axis, direction):
    length = padded.shape[axis]
    cells = length - 4

    def take(arr, start, stop):
        return lax.slice_in_dim(arr, start, stop, axis=axis)
    diff = take(padded, 1, length) - take(padded, 0, length - 1)
    slope = minmod(take(diff, 0, length - 2), take(diff, 1, length - 1))
    left = take(padded, 1, length - 2) + 0.5 * take(slope, 0, length - 3)
    right = take(padded, 2, length - 1) - 0.5 * take(slope, 1, length - 2)
    face = rusanov(left, right, direction)
    return take(face, 1, cells + 1) - take(face, 0, cells)

def sources(core):
    rho = core[0]
    zeros = jnp.zeros_like(rho)
    return jnp.stack([zeros, 2.0 * omega_rate * rho * core[2], -(2.0 - shear_rate) * omega_rate * rho * core[1], zeros, shear_rate * omega_rate * (rho * core[1] * core[2] - core[5] * core[6]), zeros, -shear_rate * omega_rate * core[5], zeros])

def section_update(block, old):
    core = block[:, :, 2:-2, 2:-2]
    radial = sweep(block[:, :, :, 2:-2], 2, 0)
    azimuthal = sweep(block[:, :, 2:-2, :], 3, 1)
    zpadded = jnp.concatenate([core[:, -2:], core, core[:, :2]], axis=1)
    vertical = sweep(zpadded, 1, 2)
    rates = -(radial + azimuthal + vertical) + sources(core)
    return 0.5 * old + 0.5 * (conserved(core) + time_step * rates)

def reference(old_state, section_prims, shear_whole, shear_frac):
    shift_cells = shear_whole[0]
    frac = shear_frac[0]
    inner_src = section_prims[:, :, NX - 2:NX, :]
    outer_src = section_prims[:, :, 0:2, :]
    inner = (1.0 - frac) * jnp.roll(inner_src, -shift_cells, axis=3) + frac * jnp.roll(inner_src, -shift_cells - 1, axis=3)
    outer = (1.0 - frac) * jnp.roll(outer_src, shift_cells, axis=3) + frac * jnp.roll(outer_src, shift_cells + 1, axis=3)
    xpadded = jnp.concatenate([inner, section_prims, outer], axis=2)
    padded = jnp.concatenate([xpadded[..., -2:], xpadded, xpadded[..., :2]], axis=3)

    def one_block(index):
        block = lax.dynamic_slice_in_dim(padded, index * CX, CX + 4, 2)
        old = lax.dynamic_slice_in_dim(old_state, index * CX, CX, 2)
        return section_update(block, old)
    blocks = lax.map(one_block, jnp.arange(N_GX, dtype=jnp.int32))
    return jnp.transpose(blocks, (1, 2, 0, 3, 4)).reshape(NF, NZ, NX, NY)
```

```python
import functools

import jax
import jax.numpy as jnp
from jax import lax
from jax.experimental import pallas as pl
from jax.experimental.pallas import tpu as pltpu
from jax.sharding import PartitionSpec as P

gamma_gas = 5.0 / 3.0
omega_rate = 1.0
shear_rate = 1.5
time_step = 0.1

FIELDS = 8
EDGE = 4


def median0(a, b):
    return jnp.maximum(jnp.minimum(a, b), jnp.minimum(jnp.maximum(a, b), 0.0))


def half_slope(a, b):
    return 0.5 * median0(a, b)


def side(w, n):
    t, u = (n + 1) % 3, (n + 2) % 3
    rho, p = w[0], w[4]
    vn, vt, vu = w[1 + n], w[1 + t], w[1 + u]
    bn, bt, bu = w[5 + n], w[5 + t], w[5 + u]
    mn, mt, mu = rho * vn, rho * vt, rho * vu
    mnvn = mn * vn
    bn2 = bn * bn
    bt2 = bt * bt + bu * bu
    bsq = bn2 + bt2
    q = 0.5 * (mnvn + mt * vt + mu * vu) + p * (1.0 / (gamma_gas - 1.0))
    pm = 0.5 * bsq
    cons = [None] * FIELDS
    flux = [None] * FIELDS
    cons[0], cons[1 + n], cons[1 + t], cons[1 + u] = rho, mn, mt, mu
    cons[4] = q + pm
    cons[5 + n], cons[5 + t], cons[5 + u] = bn, bt, bu
    flux[0] = mn
    flux[1 + n] = mnvn + (p + pm - bn2)
    flux[1 + t] = mt * vn - bt * bn
    flux[1 + u] = mu * vn - bu * bn
    flux[4] = (q + p + bt2) * vn - bn * (vt * bt + vu * bu)
    flux[5 + t] = bt * vn - vt * bn
    flux[5 + u] = bu * vn - vu * bn
    a = gamma_gas * p
    diff = a - bsq
    disc = diff * diff + (4.0 * a) * bt2
    x = a + bsq + disc * lax.rsqrt(jnp.maximum(disc, 1e-30))
    speed = jnp.abs(vn) + x * lax.rsqrt((rho + rho) * x)
    return cons, flux, speed


def twice_face(left, right, n):
    cl, fl, sl = side(left, n)
    cr, fr, sr = side(right, n)
    s = jnp.maximum(sl, sr)
    out = []
    for j in range(FIELDS):
        jump = s * (cr[j] - cl[j])
        out.append(-jump if j == 5 + n else fl[j] + fr[j] - jump)
    return out


def rows_of(ref, x, nx):
    return [ref[f, pl.ds(x, 8, stride=nx), :] for f in range(FIELDS)]


def lanes():
    return lax.broadcasted_iota(jnp.int32, (8, 128), 1)


def pack_kernel(nx, par_ref, w_ref, xa_ref, xb_ref, ye_ref):
    odd = par_ref[0]
    first_a = (1 - odd) * (nx - 2)
    first_b = odd * (nx - 2)
    for f in range(FIELDS):
        for g in range(2):
            xa_ref[f, g] = w_ref[f, pl.ds(first_a + g, 8, stride=nx), :]
            xb_ref[f, g] = w_ref[f, pl.ds(first_b + g, 8, stride=nx), :]
    group = lanes() // EDGE
    for f in range(FIELDS):
        acc = jnp.zeros((8, 128), jnp.float32)
        for x in range(nx):
            row = w_ref[f, pl.ds(x, 8, stride=nx), :]
            acc = jnp.where(group == x, pltpu.roll(row, (EDGE * x + 2) % 128, 1), acc)
        ye_ref[f] = acc


def inner_kernel(nx, w_ref, old_ref, acc_ref, g_ref):
    def finish(x, div):
        w = rows_of(w_ref, x, nx)
        old = rows_of(old_ref, x, nx)
        rho, vx, vy, vz, p, bx, by, bz = w
        mx, my, mz = rho * vx, rho * vy, rho * vz
        energy = (
            p * (1.0 / (gamma_gas - 1.0))
            + 0.5 * (mx * vx + my * vy + mz * vz)
            + 0.5 * (bx * bx + by * by + bz * bz)
        )
        cons = [rho, mx, my, mz, energy, bx, by, bz]
        half_dt = 0.5 * time_step
        src = [None] * FIELDS
        src[1] = (half_dt * 2.0 * omega_rate) * my
        src[2] = (-half_dt * (2.0 - shear_rate) * omega_rate) * mx
        src[4] = (half_dt * shear_rate * omega_rate) * (mx * vy - bx * by)
        src[6] = (-half_dt * shear_rate * omega_rate) * bx
        for f in range(FIELDS):
            total = 0.5 * (old[f] + cons[f]) + (0.5 * half_dt) * div[f]
            acc_ref[f, x] = total if src[f] is None else total + src[f]

    def vertical(x):
        w = rows_of(w_ref, x, nx)
        left, right = [], []
        for f in range(FIELDS):
            up = pltpu.roll(w[f], 7, 0) - w[f]
            h = half_slope(pltpu.roll(up, 1, 0), up)
            left.append(w[f] + h)
            right.append(pltpu.roll(w[f] - h, 7, 0))
        g = twice_face(left, right, 2)
        return [pltpu.roll(v, 1, 0) - v for v in g]

    def radial(x):
        w0 = rows_of(w_ref, x - 1, nx)
        w1 = rows_of(w_ref, x, nx)
        w2 = rows_of(w_ref, x + 1, nx)
        w3 = rows_of(w_ref, x + 2, nx)
        left, right = [], []
        for f in range(FIELDS):
            mid = w2[f] - w1[f]
            left.append(w1[f] + half_slope(w1[f] - w0[f], mid))
            right.append(w2[f] - half_slope(mid, w3[f] - w2[f]))
        return twice_face(left, right, 0)

    finish(0, vertical(0))
    for f in range(FIELDS):
        g_ref[f] = jnp.zeros((8, 128), jnp.float32)

    def body(x, _):
        div = vertical(x)
        g = radial(x)
        for f in range(FIELDS):
            div[f] = div[f] + (g_ref[f] - g[f])
            g_ref[f] = g[f]
        finish(x, div)
        return 0

    lax.fori_loop(1, nx - 2, body, 0)
    div = vertical(nx - 2)
    finish(nx - 2, [div[f] + g_ref[f] for f in range(FIELDS)])
    finish(nx - 1, vertical(nx - 1))


def outer_kernel(
    nx, num_ref, frac_ref, w_ref, acc_ref, ye_ref, c_ref, y_ref, xa_ref, xb_ref, xe_ref,
    out_ref, h_ref, q_ref, x_ref, d_ref,
):
    odd_x, odd_y, shift, inner, outer = (num_ref[i] for i in range(5))
    frac = frac_ref[0]
    lane = lanes()
    scale = 0.25 * time_step

    ends = inner + outer
    frac = jnp.where(ends == 1, frac, 0.0)

    def window(b, e, s):
        amount = jnp.where(inner == 1, lax.rem(128 - s, 128), jnp.where(outer == 1, lax.rem(s, 128), 0))
        low = jnp.where(outer == 1, s, 0)
        high = jnp.where(inner == 1, 128 - s, 128)
        near = (lane >= low) & (lane < high)
        return jnp.where(near, pltpu.roll(b, amount, 1), pltpu.roll(e, amount, 1))

    for f in range(FIELDS):
        for g in range(2):
            b, e = xb_ref[f, g], xe_ref[f, g]
            ghost = (1.0 - frac) * window(b, e, shift) + frac * window(b, e, shift + 1)
            own = xa_ref[f, g]
            x_ref[f, g] = jnp.where(odd_x == 1, own, ghost)
            x_ref[f, 2 + g] = jnp.where(odd_x == 1, ghost, own)

    def radial(w0, w1, w2, w3):
        left, right = [], []
        for f in range(FIELDS):
            mid = w2[f] - w1[f]
            left.append(w1[f] + half_slope(w1[f] - w0[f], mid))
            right.append(w2[f] - half_slope(mid, w3[f] - w2[f]))
        return twice_face(left, right, 0)

    def ghosts(i):
        return [x_ref[f, i] for f in range(FIELDS)]

    def rows(x):
        return rows_of(w_ref, x, nx)

    for i, x in ((0, 0), (2, nx - 2)):
        if i == 0:
            strip = [ghosts(0), ghosts(1), rows(0), rows(1), rows(2)]
        else:
            strip = [rows(nx - 3), rows(nx - 2), rows(nx - 1), ghosts(2), ghosts(3)]
        g0 = radial(*strip[:4])
        g1 = radial(*strip[1:])
        for f in range(FIELDS):
            if i == 0:
                d_ref[f, 0] = g0[f] - g1[f]
                d_ref[f, 1] = g1[f]
            else:
                d_ref[f, 2] = -g0[f]
                d_ref[f, 3] = g0[f] - g1[f]

    place = lax.rem(lane, EDGE)
    from_left = place < 2
    left, right, outside = [], [], []
    for f in range(FIELDS):
        own = ye_ref[f]
        core, cross = c_ref[f], y_ref[f]
        near = jnp.where(odd_y == 1, core, cross)
        far = jnp.where(odd_y == 1, cross, core)
        h = jnp.where(from_left, near, far)
        h_ref[f] = h
        w0 = jnp.where(place == 1, pltpu.roll(h, 1, 1), pltpu.roll(own, 2, 1))
        w1 = jnp.where(place == 1, h, pltpu.roll(own, 1, 1))
        w2 = jnp.where(place == 1, pltpu.roll(own, 127, 1), h)
        w3 = jnp.where(place == 1, pltpu.roll(own, 126, 1), pltpu.roll(h, 127, 1))
        mid = w2 - w1
        left.append(w1 + half_slope(w1 - w0, mid))
        r = w2 - half_slope(mid, w3 - w2)
        right.append(r)
        outside.append(r)
    g = twice_face(left, right, 1)
    for f in range(FIELDS):
        q_ref[f] = g[f]

    def body(x, _):
        w = rows_of(w_ref, x, nx)
        turn = lax.rem(126 - EDGE * x + 512, 128)
        edge_turn = lax.rem(126 - EDGE * x + 512, 128)
        left, right = [], []
        for f in range(FIELDS):
            h = pltpu.roll(h_ref[f], turn, 1)
            up = pltpu.roll(jnp.where(lane == 0, h, w[f]), 127, 1) - w[f]
            down = w[f] - pltpu.roll(jnp.where(lane == 127, h, w[f]), 1, 1)
            s = half_slope(down, up)
            left.append(w[f] + s)
            right.append(pltpu.roll(w[f] - s, 127, 1))
        g = twice_face(left, right, 1)
        for f in range(FIELDS):
            q = pltpu.roll(q_ref[f], edge_turn, 1)
            lower = pltpu.roll(jnp.where(lane == 127, q, g[f]), 1, 1)
            upper = jnp.where(lane == 127, pltpu.roll(q, 127, 1), g[f])
            out_ref[f, pl.ds(x, 8, stride=nx), :] = acc_ref[f, x] + scale * (lower - upper)
        return 0

    lax.fori_loop(0, nx, body, 0)
    for i, x in ((0, 0), (1, 1), (2, nx - 2), (3, nx - 1)):
        for f in range(FIELDS):
            at = (f, pl.ds(x, 8, stride=nx), slice(None))
            out_ref[at] = out_ref[at] + scale * d_ref[f, i]


def swaps(nx, ny):
    def at(g, j):
        return (g % nx) * ny + j % ny

    grid = [(g, j) for g in range(nx) for j in range(ny)]
    core = [(at(g, j), at(g, j ^ 1)) for g, j in grid]
    cross = [(at(g, j), at(g, j + 1 if j % 2 else j - 1)) for g, j in grid]
    along = [(at(g, j), at(g ^ 1, j)) for g, j in grid]

    def ends(k):
        there = [(at(0, j), at(nx - 1, j + k)) for j in range(ny)]
        return there + [(b, a) for a, b in there]

    def other(k):
        inside = [(at(g, j), at(g + 1 if g % 2 else g - 1, j)) for g, j in grid if 0 < g < nx - 1]
        return inside + ends(k)

    return core, cross, along, other, ends


def on_device(old_state, section_prims, shear_whole, shear_frac):
    n_gx, n_gy = lax.axis_size("gx"), lax.axis_size("gy")
    gx, gy = lax.axis_index("gx"), lax.axis_index("gy")
    fields, nz, nx, cells = section_prims.shape
    assert (fields, nz, cells) == (FIELDS, 8, 128)
    assert EDGE * nx == cells and n_gx % 2 == 0 and n_gy % 2 == 0
    axes = ("gx", "gy")
    core, cross, along, other, ends = swaps(n_gx, n_gy)
    w = section_prims.reshape(fields, nz * nx, cells)
    old = old_state.reshape(fields, nz * nx, cells)
    f32 = jnp.float32
    vmem = pl.BlockSpec(memory_space=pltpu.VMEM)
    smem = pl.BlockSpec(memory_space=pltpu.SMEM)
    edge_rows = jax.ShapeDtypeStruct((fields, 2, nz, cells), f32)

    odd_x, odd_y = lax.rem(gx, 2), lax.rem(gy, 2)
    xa, xb, ye = pl.pallas_call(
        functools.partial(pack_kernel, nx),
        out_shape=(edge_rows, edge_rows, jax.ShapeDtypeStruct((fields, nz, cells), f32)),
        in_specs=[smem, vmem],
        out_specs=(vmem, vmem, vmem),
        name="pack",
    )(odd_x[None].astype(jnp.int32), w)

    c_in = lax.ppermute(ye, axes, core)
    y_in = lax.ppermute(ye, axes, cross)
    xa_in = lax.ppermute(xa, axes, along)

    def branch(k):
        def run(xb, w, old):
            xb_in = lax.ppermute(xb, axes, other(k))
            xe_in = lax.ppermute(xb, axes, ends(k + 1))
            acc = pl.pallas_call(
                functools.partial(inner_kernel, nx),
                out_shape=jax.ShapeDtypeStruct((fields, nx, nz, cells), f32),
                in_specs=[vmem, vmem],
                out_specs=vmem,
                scratch_shapes=[pltpu.VMEM((fields, nz, cells), f32)],
                cost_estimate=pl.CostEstimate(
                    flops=480 * nx * nz * cells, bytes_accessed=12 * fields * nx * nz * cells, transcendentals=0
                ),
                name="inner",
            )(w, old)
            return xb_in, xe_in, acc

        return run

    whole = lax.rem(shear_whole[0] // cells, n_gy)
    xb_in, xe_in, acc = lax.switch(whole, [branch(k) for k in range(n_gy)], xb, w, old)

    numbers = jnp.stack(
        [
            odd_x,
            odd_y,
            lax.rem(shear_whole[0], cells),
            (gx == 0).astype(jnp.int32),
            (gx == n_gx - 1).astype(jnp.int32),
        ]
    ).astype(jnp.int32)
    tile = (fields, nz, cells)
    out = pl.pallas_call(
        functools.partial(outer_kernel, nx),
        out_shape=jax.ShapeDtypeStruct((fields, nz * nx, cells), f32),
        in_specs=[smem, smem] + [vmem] * 8,
        out_specs=vmem,
        scratch_shapes=[
            pltpu.VMEM(tile, f32),
            pltpu.VMEM(tile, f32),
            pltpu.VMEM((fields, 4, nz, cells), f32),
            pltpu.VMEM((fields, 4, nz, cells), f32),
        ],
        name="outer",
    )(numbers, shear_frac, w, acc, ye, c_in, y_in, xa_in, xb_in, xe_in)
    return out.reshape(section_prims.shape)


def solution(mesh):
    in_specs = (P(None, None, "gx", "gy"), P(None, None, "gx", "gy"), P(), P())
    out_specs = P(None, None, "gx", "gy")
    return jax.shard_map(
        on_device, mesh=mesh, in_specs=in_specs, out_specs=out_specs, check_vma=False
    )
```

```python
import functools

import jax
import jax.numpy as jnp
from jax import lax
from jax.experimental import pallas as pl
from jax.experimental.pallas import tpu as pltpu
from jax.sharding import PartitionSpec as P

gamma_gas = 5.0 / 3.0
omega_rate = 1.0
shear_rate = 1.5
time_step = 0.1

FIELDS = 8
EDGE = 8
ROWS = 128 // EDGE


def median0(a, b):
    return jnp.maximum(jnp.minimum(a, b), jnp.minimum(jnp.maximum(a, b), 0.0))


def half_slope(a, b):
    return 0.5 * median0(a, b)


def side(w, n):
    t, u = (n + 1) % 3, (n + 2) % 3
    rho, p = w[0], w[4]
    vn, vt, vu = w[1 + n], w[1 + t], w[1 + u]
    bn, bt, bu = w[5 + n], w[5 + t], w[5 + u]
    mn, mt, mu = rho * vn, rho * vt, rho * vu
    mnvn = mn * vn
    bn2 = bn * bn
    bt2 = bt * bt + bu * bu
    bsq = bn2 + bt2
    q = 0.5 * (mnvn + mt * vt + mu * vu) + p * (1.0 / (gamma_gas - 1.0))
    pm = 0.5 * bsq
    cons = [None] * FIELDS
    flux = [None] * FIELDS
    cons[0], cons[1 + n], cons[1 + t], cons[1 + u] = rho, mn, mt, mu
    cons[4] = q + pm
    cons[5 + n], cons[5 + t], cons[5 + u] = bn, bt, bu
    flux[0] = mn
    flux[1 + n] = mnvn + (p + pm - bn2)
    flux[1 + t] = mt * vn - bt * bn
    flux[1 + u] = mu * vn - bu * bn
    flux[4] = (q + p + bt2) * vn - bn * (vt * bt + vu * bu)
    flux[5 + t] = bt * vn - vt * bn
    flux[5 + u] = bu * vn - vu * bn
    a = gamma_gas * p
    diff = a - bsq
    disc = diff * diff + (4.0 * a) * bt2
    x = a + bsq + disc * lax.rsqrt(jnp.maximum(disc, 1e-30))
    speed = jnp.abs(vn) + x * lax.rsqrt((rho + rho) * x)
    return cons, flux, speed


def twice_face(left, right, n):
    cl, fl, sl = side(left, n)
    cr, fr, sr = side(right, n)
    s = jnp.maximum(sl, sr)
    out = []
    for j in range(FIELDS):
        jump = s * (cr[j] - cl[j])
        out.append(-jump if j == 5 + n else fl[j] + fr[j] - jump)
    return out


def lanes():
    return lax.broadcasted_iota(jnp.int32, (8, 128), 1)


def rows_of(ref, x):
    return [ref[f, x] for f in range(FIELDS)]


def transposing(src, dst, sem):
    return [pltpu.make_async_copy(src.at[:, z], dst.at[:, :, z], sem.at[z]) for z in range(8)]


def pack_kernel(nx, w_ref, wt_ref, xa_ref, xb_ref, ye_ref, sem):
    copies = transposing(w_ref, wt_ref, sem)
    for copy in copies:
        copy.start()
    odd = lax.rem(lax.axis_index("gx"), 2)
    first_a = (1 - odd) * (nx - 2)
    first_b = odd * (nx - 2)
    group = lanes() // EDGE
    for copy in copies:
        copy.wait()
    for f in range(FIELDS):
        for g in range(2):
            xa_ref[f, g] = wt_ref[f, first_a + g]
            xb_ref[f, g] = wt_ref[f, first_b + g]
    for f in range(FIELDS):
        for v in range(nx // ROWS):
            acc = jnp.zeros((8, 128), jnp.float32)
            for i in range(ROWS):
                row = wt_ref[f, v * ROWS + i]
                acc = jnp.where(group == i, pltpu.roll(row, (EDGE * i + 4) % 128, 1), acc)
            ye_ref[f, v] = acc


def inner_kernel(
    nx, wt_ref, old_ref, acc_ref, old_t, g_ref, l_ref, d_ref, al_ref, am_ref, ar_ref, ag_ref, sem
):
    copies = transposing(old_ref, old_t, sem)
    for copy in copies:
        copy.start()
    lane = lanes()
    whole = (lane > 0) & (lane < 126)

    def finish(x, w, div):
        rho, vx, vy, vz, p, bx, by, bz = w
        mx, my, mz = rho * vx, rho * vy, rho * vz
        energy = (
            p * (1.0 / (gamma_gas - 1.0))
            + 0.5 * (mx * vx + my * vy + mz * vz)
            + 0.5 * (bx * bx + by * by + bz * bz)
        )
        cons = [rho, mx, my, mz, energy, bx, by, bz]
        half_dt = 0.5 * time_step
        src = [None] * FIELDS
        src[1] = (half_dt * 2.0 * omega_rate) * my
        src[2] = (-half_dt * (2.0 - shear_rate) * omega_rate) * mx
        src[4] = (half_dt * shear_rate * omega_rate) * (mx * vy - bx * by)
        src[6] = (-half_dt * shear_rate * omega_rate) * bx
        for f in range(FIELDS):
            total = 0.5 * cons[f] + (0.5 * half_dt) * div[f]
            acc_ref[f, x] = total if src[f] is None else total + src[f]

    def vertical(w):
        left, right = [], []
        for f in range(FIELDS):
            up = pltpu.roll(w[f], 7, 0) - w[f]
            h = half_slope(pltpu.roll(up, 1, 0), up)
            left.append(w[f] + h)
            right.append(pltpu.roll(w[f] - h, 7, 0))
        g = twice_face(left, right, 2)
        return [pltpu.roll(v, 1, 0) - v for v in g]

    def radial(x):
        w2 = rows_of(wt_ref, jnp.minimum(x + 1, nx - 1))
        w3 = rows_of(wt_ref, jnp.minimum(x + 2, nx - 1))
        left, right = [], []
        for f in range(FIELDS):
            step = w3[f] - w2[f]
            h = half_slope(d_ref[f], step)
            left.append(l_ref[f])
            right.append(w2[f] - h)
            l_ref[f] = w2[f] + h
            d_ref[f] = step
        keep = jnp.where((x > 0) & (x < nx - 2), 1.0, 0.0)
        return [keep * v for v in twice_face(left, right, 0)]

    def states(x):
        for f in range(FIELDS):
            w = wt_ref[f, x]
            h = half_slope(w - pltpu.roll(w, 1, 1), pltpu.roll(w, 127, 1) - w)
            al_ref[f, x] = w + h
            am_ref[f, x] = w - h

    def turn(x):
        for f in range(FIELDS):
            ar_ref[f, x] = pltpu.roll(am_ref[f, x], 127, 1)

    def faces(x):
        g = twice_face(rows_of(al_ref, x), rows_of(ar_ref, x), 1)
        for f in range(FIELDS):
            ag_ref[f, x] = jnp.where(whole, g[f], 0.0)

    states(0)
    states(1)
    states(2)
    turn(0)
    turn(1)
    faces(0)
    for f in range(FIELDS):
        g_ref[f] = jnp.zeros((8, 128), jnp.float32)
        l_ref[f] = wt_ref[f, 0]
        d_ref[f] = wt_ref[f, 1] - wt_ref[f, 0]

    def body(x, _):
        w = rows_of(wt_ref, x)
        along = rows_of(ag_ref, x)
        along = [pltpu.roll(v, 1, 1) - v for v in along]
        faces(jnp.minimum(x + 1, nx - 1))
        turn(jnp.minimum(x + 2, nx - 1))
        states(jnp.minimum(x + 3, nx - 1))
        div = vertical(w)
        g = radial(x)
        for f in range(FIELDS):
            div[f] = div[f] + (g_ref[f] - g[f]) + along[f]
            g_ref[f] = g[f]
        finish(x, w, div)
        return 0

    lax.fori_loop(0, nx, body, 0)
    for copy in copies:
        copy.wait()

    def add(x, _):
        for f in range(FIELDS):
            acc_ref[f, x] = acc_ref[f, x] + 0.5 * old_t[f, x]
        return 0

    lax.fori_loop(0, nx, add, 0)


def outer_kernel(
    nx, whole_ref, frac_ref, wt_ref, acc_ref, ye_ref, c_ref, y_ref, xa_ref, xb_ref, xe_ref,
    out_ref, new_ref, q_ref, x_ref, d_ref, sem,
):
    gx, gy = lax.axis_index("gx"), lax.axis_index("gy")
    odd_x, odd_y = lax.rem(gx, 2), lax.rem(gy, 2)
    inner = gx == 0
    outer = gx == lax.axis_size("gx") - 1
    shift = lax.rem(whole_ref[0], 128)
    frac = jnp.where(inner | outer, frac_ref[0], 0.0)
    lane = lanes()
    scale = 0.25 * time_step

    def window(b, e, s):
        amount = jnp.where(inner, lax.rem(128 - s, 128), jnp.where(outer, lax.rem(s, 128), 0))
        low = jnp.where(outer, s, 0)
        high = jnp.where(inner, 128 - s, 128)
        near = (lane >= low) & (lane < high)
        return jnp.where(near, pltpu.roll(b, amount, 1), pltpu.roll(e, amount, 1))

    for f in range(FIELDS):
        for g in range(2):
            b, e = xb_ref[f, g], xe_ref[f, g]
            ghost = (1.0 - frac) * window(b, e, shift) + frac * window(b, e, shift + 1)
            own = xa_ref[f, g]
            x_ref[f, g] = jnp.where(odd_x == 1, own, ghost)
            x_ref[f, 2 + g] = jnp.where(odd_x == 1, ghost, own)

    def radial(w0, w1, w2, w3):
        left, right = [], []
        for f in range(FIELDS):
            mid = w2[f] - w1[f]
            left.append(w1[f] + half_slope(w1[f] - w0[f], mid))
            right.append(w2[f] - half_slope(mid, w3[f] - w2[f]))
        return twice_face(left, right, 0)

    place = lax.rem(lane, EDGE)
    low = place < 4
    for v in range(nx // ROWS):
        left, right = [], []
        for f in range(FIELDS):
            own, core, cross = ye_ref[f, v], c_ref[f, v], y_ref[f, v]
            before = jnp.where(odd_y == 1, core, cross)
            after = jnp.where(odd_y == 1, cross, core)
            end = jnp.where(low, own, after)
            start = jnp.where(low, before, own)
            w0 = jnp.where(low, pltpu.roll(end, 1, 1), pltpu.roll(start, 2, 1))
            w1 = jnp.where(low, end, pltpu.roll(start, 1, 1))
            w2 = jnp.where(low, pltpu.roll(end, 127, 1), start)
            w3 = jnp.where(low, pltpu.roll(end, 126, 1), pltpu.roll(start, 127, 1))
            mid = w2 - w1
            left.append(w1 + half_slope(w1 - w0, mid))
            right.append(w2 - half_slope(mid, w3 - w2))
        g = twice_face(left, right, 1)
        for f in range(FIELDS):
            lower = jnp.where(low, jnp.where(place == 3, pltpu.roll(g[f], 1, 1), 0.0), g[f])
            upper = jnp.where(low, g[f], jnp.where(place == 4, pltpu.roll(g[f], 127, 1), 0.0))
            q_ref[f, v] = scale * (lower - upper)

    def ghosts(i):
        return [x_ref[f, i] for f in range(FIELDS)]

    def rows(x):
        return rows_of(wt_ref, x)

    g0 = radial(ghosts(0), ghosts(1), rows(0), rows(1))
    g1 = radial(ghosts(1), rows(0), rows(1), rows(2))
    for f in range(FIELDS):
        d_ref[f, 0] = scale * (g0[f] - g1[f])
        d_ref[f, 1] = scale * g1[f]
    g0 = radial(rows(nx - 3), rows(nx - 2), rows(nx - 1), ghosts(2))
    g1 = radial(rows(nx - 2), rows(nx - 1), ghosts(2), ghosts(3))
    for f in range(FIELDS):
        d_ref[f, 2] = -scale * g0[f]
        d_ref[f, 3] = scale * (g0[f] - g1[f])

    edge = (lane < 2) | (lane > 125)
    copies = []
    for f in range(FIELDS):
        for x in range(nx):
            q = pltpu.roll(q_ref[f, x // ROWS], (124 - EDGE * (x % ROWS)) % 128, 1)
            new = acc_ref[f, x] + jnp.where(edge, q, 0.0)
            at = {0: 0, 1: 1, nx - 2: 2, nx - 1: 3}.get(x)
            new_ref[f, x] = new if at is None else new + d_ref[f, at]
        for z in range(8):
            copy = pltpu.make_async_copy(new_ref.at[f, :, z], out_ref.at[f, z], sem.at[f, z])
            copy.start()
            copies.append(copy)
    for copy in copies:
        copy.wait()


def swaps(nx, ny):
    def at(g, j):
        return (g % nx) * ny + j % ny

    grid = [(g, j) for g in range(nx) for j in range(ny)]
    core = [(at(g, j), at(g, j ^ 1)) for g, j in grid]
    cross = [(at(g, j), at(g, j + 1 if j % 2 else j - 1)) for g, j in grid]
    along = [(at(g, j), at(g ^ 1, j)) for g, j in grid]

    def ends(k):
        there = [(at(0, j), at(nx - 1, j + k)) for j in range(ny)]
        return there + [(b, a) for a, b in there]

    def other(k):
        inside = [(at(g, j), at(g + 1 if g % 2 else g - 1, j)) for g, j in grid if 0 < g < nx - 1]
        return inside + ends(k)

    return core, cross, along, other, ends


def on_device(old_state, section_prims, shear_whole, shear_frac):
    n_gx, n_gy = lax.axis_size("gx"), lax.axis_size("gy")
    gx, gy = lax.axis_index("gx"), lax.axis_index("gy")
    fields, nz, nx, cells = section_prims.shape
    assert (fields, nz, cells) == (FIELDS, 8, 128)
    assert nx % ROWS == 0 and n_gx % 2 == 0 and n_gy % 2 == 0
    axes = ("gx", "gy")
    core, cross, along, other, ends = swaps(n_gx, n_gy)
    f32 = jnp.float32
    vmem = pl.BlockSpec(memory_space=pltpu.VMEM)
    smem = pl.BlockSpec(memory_space=pltpu.SMEM)
    hbm = pl.BlockSpec(memory_space=pltpu.HBM)
    block = (fields, nx, nz, cells)
    tile = (fields, nz, cells)
    packed = (fields, nx // ROWS, nz, cells)
    edge_rows = jax.ShapeDtypeStruct((fields, 2, nz, cells), f32)

    wt, xa, xb, ye = pl.pallas_call(
        functools.partial(pack_kernel, nx),
        out_shape=(
            jax.ShapeDtypeStruct(block, f32),
            edge_rows,
            edge_rows,
            jax.ShapeDtypeStruct(packed, f32),
        ),
        in_specs=[hbm],
        out_specs=(vmem,) * 4,
        scratch_shapes=[pltpu.SemaphoreType.DMA((nz,))],
        name="pack",
    )(section_prims)

    c_in = lax.ppermute(ye, axes, core)
    y_in = lax.ppermute(ye, axes, cross)
    xa_in = lax.ppermute(xa, axes, along)

    def branch(k):
        def run(xb, wt, old):
            xb_in = lax.ppermute(xb, axes, other(k))
            xe_in = lax.ppermute(xb, axes, ends(k + 1))
            acc = pl.pallas_call(
                functools.partial(inner_kernel, nx),
                out_shape=jax.ShapeDtypeStruct(block, f32),
                in_specs=[vmem, hbm],
                out_specs=vmem,
                scratch_shapes=[pltpu.VMEM(block, f32)]
                + [pltpu.VMEM(tile, f32)] * 3
                + [pltpu.VMEM(block, f32)] * 4
                + [pltpu.SemaphoreType.DMA((nz,))],
                cost_estimate=pl.CostEstimate(
                    flops=720 * nx * nz * cells, bytes_accessed=12 * fields * nx * nz * cells, transcendentals=0
                ),
                name="inner",
            )(wt, old)
            return xb_in, xe_in, acc

        return run

    whole = lax.rem(shear_whole[0] // cells, n_gy)
    xb_in, xe_in, acc = lax.switch(whole, [branch(k) for k in range(n_gy)], xb, wt, old_state)

    return pl.pallas_call(
        functools.partial(outer_kernel, nx),
        out_shape=jax.ShapeDtypeStruct(section_prims.shape, f32),
        in_specs=[smem, smem] + [vmem] * 8,
        out_specs=hbm,
        scratch_shapes=[
            pltpu.VMEM(block, f32),
            pltpu.VMEM(packed, f32),
            pltpu.VMEM((fields, 4, nz, cells), f32),
            pltpu.VMEM((fields, 4, nz, cells), f32),
            pltpu.SemaphoreType.DMA((fields, nz)),
        ],
        name="outer",
    )(shear_whole, shear_frac, wt, acc, ye, c_in, y_in, xa_in, xb_in, xe_in)


def solution(mesh):
    in_specs = (P(None, None, "gx", "gy"), P(None, None, "gx", "gy"), P(), P())
    out_specs = P(None, None, "gx", "gy")
    return jax.shard_map(
        on_device, mesh=mesh, in_specs=in_specs, out_specs=out_specs, check_vma=False
    )
```

```python
import functools

import jax
import jax.numpy as jnp
from jax import lax
from jax.experimental import pallas as pl
from jax.experimental.pallas import tpu as pltpu
from jax.sharding import PartitionSpec as P

gamma_gas = 5.0 / 3.0
omega_rate = 1.0
shear_rate = 1.5
time_step = 0.1

FIELDS = 8
EDGE = 8
ROWS = 128 // EDGE


def median0(a, b):
    return jnp.maximum(jnp.minimum(a, b), jnp.minimum(jnp.maximum(a, b), 0.0))


def half_slope(a, b):
    return 0.5 * median0(a, b)


def side(w, n):
    t, u = (n + 1) % 3, (n + 2) % 3
    rho, p = w[0], w[4]
    vn, vt, vu = w[1 + n], w[1 + t], w[1 + u]
    bn, bt, bu = w[5 + n], w[5 + t], w[5 + u]
    mn, mt, mu = rho * vn, rho * vt, rho * vu
    mnvn = mn * vn
    bn2 = bn * bn
    bt2 = bt * bt + bu * bu
    bsq = bn2 + bt2
    q = 0.5 * (mnvn + mt * vt + mu * vu) + p * (1.0 / (gamma_gas - 1.0))
    pm = 0.5 * bsq
    cons = [None] * FIELDS
    flux = [None] * FIELDS
    cons[0], cons[1 + n], cons[1 + t], cons[1 + u] = rho, mn, mt, mu
    cons[4] = q + pm
    cons[5 + n], cons[5 + t], cons[5 + u] = bn, bt, bu
    flux[0] = mn
    flux[1 + n] = mnvn + (p + pm - bn2)
    flux[1 + t] = mt * vn - bt * bn
    flux[1 + u] = mu * vn - bu * bn
    flux[4] = (q + p + bt2) * vn - bn * (vt * bt + vu * bu)
    flux[5 + t] = bt * vn - vt * bn
    flux[5 + u] = bu * vn - vu * bn
    a = gamma_gas * p
    diff = a - bsq
    disc = diff * diff + (4.0 * a) * bt2
    x = a + bsq + disc * lax.rsqrt(jnp.maximum(disc, 1e-30))
    speed = jnp.abs(vn) + x * lax.rsqrt((rho + rho) * x)
    return cons, flux, speed


def twice_face(left, right, n):
    cl, fl, sl = side(left, n)
    cr, fr, sr = side(right, n)
    s = jnp.maximum(sl, sr)
    out = []
    for j in range(FIELDS):
        jump = s * (cr[j] - cl[j])
        out.append(-jump if j == 5 + n else fl[j] + fr[j] - jump)
    return out


def lanes():
    return lax.broadcasted_iota(jnp.int32, (8, 128), 1)


def rows_of(ref, x):
    return [ref[f, x] for f in range(FIELDS)]


def transposing(src, dst, sem):
    return [pltpu.make_async_copy(src.at[:, z], dst.at[:, :, z], sem.at[z]) for z in range(8)]


def pack_kernel(
    nx, whole_hbm, frac_hbm, w_ref, wt_ref, xa_ref, ex_ref, k_ref, shift_ref, frac_ref,
    whole_ref, frac_in, sem, scalar_sem,
):
    copies = transposing(w_ref, wt_ref, sem)
    copies.append(pltpu.make_async_copy(whole_hbm, whole_ref, scalar_sem.at[0]))
    copies.append(pltpu.make_async_copy(frac_hbm, frac_in, scalar_sem.at[1]))
    for copy in copies:
        copy.start()
    odd = lax.rem(lax.axis_index("gx"), 2)
    first_a = (1 - odd) * (nx - 2)
    first_b = odd * (nx - 2)
    group = lanes() // EDGE
    tiles = nx // ROWS
    for copy in copies:
        copy.wait()
    k_ref[0] = lax.rem(whole_ref[0] // 128, lax.axis_size("gy"))
    shift_ref[0] = lax.rem(whole_ref[0], 128)
    frac_ref[0] = frac_in[0]
    for f in range(FIELDS):
        for g in range(2):
            xa_ref[f, g] = wt_ref[f, first_a + g]
            ex_ref[f, tiles + g] = wt_ref[f, first_b + g]
    for f in range(FIELDS):
        for v in range(tiles):
            acc = jnp.zeros((8, 128), jnp.float32)
            for i in range(ROWS):
                row = wt_ref[f, v * ROWS + i]
                acc = jnp.where(group == i, pltpu.roll(row, (EDGE * i + 4) % 128, 1), acc)
            ex_ref[f, v] = acc


def shear_kernel(nx, shift_ref, frac_ref, ex_ref, c_ref, y_ref, xb_ref):
    gx, odd_y = lax.axis_index("gx"), lax.rem(lax.axis_index("gy"), 2)
    upper = gx == lax.axis_size("gx") - 1
    end = upper | (gx == 0)
    shift = jnp.where(end, shift_ref[0], 0)
    frac = jnp.where(end, frac_ref[0], 0.0)
    sibling = (odd_y == 1) != upper
    lane = lanes()
    tiles = nx // ROWS

    def window(own, other, s):
        amount = jnp.where(upper, lax.rem(128 - s, 128), lax.rem(s, 128))
        low = jnp.where(upper, 0, s)
        high = jnp.where(upper, 128 - s, 128)
        near = (lane >= low) & (lane < high)
        return pltpu.roll(own, amount, 1), pltpu.roll(other, amount, 1), near

    for f in range(FIELDS):
        for g in range(2):
            own = ex_ref[f, tiles + g]
            other = jnp.where(sibling, c_ref[f, tiles + g], y_ref[f, tiles + g])
            a, b, near = window(own, other, shift)
            first = jnp.where(near, a, b)
            a, b, near = window(own, other, shift + 1)
            second = jnp.where(near, a, b)
            xb_ref[f, g] = (1.0 - frac) * first + frac * second


def inner_kernel(
    nx, wt_ref, old_ref, acc_ref, old_t, g_ref, l_ref, d_ref, al_ref, am_ref, ar_ref, ag_ref, sem
):
    copies = transposing(old_ref, old_t, sem)
    for copy in copies:
        copy.start()
    lane = lanes()
    whole = (lane > 0) & (lane < 126)

    def finish(x, w, div):
        rho, vx, vy, vz, p, bx, by, bz = w
        mx, my, mz = rho * vx, rho * vy, rho * vz
        energy = (
            p * (1.0 / (gamma_gas - 1.0))
            + 0.5 * (mx * vx + my * vy + mz * vz)
            + 0.5 * (bx * bx + by * by + bz * bz)
        )
        cons = [rho, mx, my, mz, energy, bx, by, bz]
        half_dt = 0.5 * time_step
        src = [None] * FIELDS
        src[1] = (half_dt * 2.0 * omega_rate) * my
        src[2] = (-half_dt * (2.0 - shear_rate) * omega_rate) * mx
        src[4] = (half_dt * shear_rate * omega_rate) * (mx * vy - bx * by)
        src[6] = (-half_dt * shear_rate * omega_rate) * bx
        for f in range(FIELDS):
            total = 0.5 * cons[f] + (0.5 * half_dt) * div[f]
            acc_ref[f, x] = total if src[f] is None else total + src[f]

    def vertical(w):
        left, right = [], []
        for f in range(FIELDS):
            up = pltpu.roll(w[f], 7, 0) - w[f]
            h = half_slope(pltpu.roll(up, 1, 0), up)
            left.append(w[f] + h)
            right.append(pltpu.roll(w[f] - h, 7, 0))
        g = twice_face(left, right, 2)
        return [pltpu.roll(v, 1, 0) - v for v in g]

    def radial(x):
        w2 = rows_of(wt_ref, jnp.minimum(x + 1, nx - 1))
        w3 = rows_of(wt_ref, jnp.minimum(x + 2, nx - 1))
        left, right = [], []
        for f in range(FIELDS):
            step = w3[f] - w2[f]
            h = half_slope(d_ref[f], step)
            left.append(l_ref[f])
            right.append(w2[f] - h)
            l_ref[f] = w2[f] + h
            d_ref[f] = step
        keep = jnp.where((x > 0) & (x < nx - 2), 1.0, 0.0)
        return [keep * v for v in twice_face(left, right, 0)]

    def states(x):
        for f in range(FIELDS):
            w = wt_ref[f, x]
            h = half_slope(w - pltpu.roll(w, 1, 1), pltpu.roll(w, 127, 1) - w)
            al_ref[f, x] = w + h
            am_ref[f, x] = w - h

    def turn(x):
        for f in range(FIELDS):
            ar_ref[f, x] = pltpu.roll(am_ref[f, x], 127, 1)

    def faces(x):
        g = twice_face(rows_of(al_ref, x), rows_of(ar_ref, x), 1)
        for f in range(FIELDS):
            ag_ref[f, x] = jnp.where(whole, g[f], 0.0)

    states(0)
    states(1)
    states(2)
    turn(0)
    turn(1)
    faces(0)
    for f in range(FIELDS):
        g_ref[f] = jnp.zeros((8, 128), jnp.float32)
        l_ref[f] = wt_ref[f, 0]
        d_ref[f] = wt_ref[f, 1] - wt_ref[f, 0]

    def body(x, _):
        w = rows_of(wt_ref, x)
        along = rows_of(ag_ref, x)
        along = [pltpu.roll(v, 1, 1) - v for v in along]
        faces(jnp.minimum(x + 1, nx - 1))
        turn(jnp.minimum(x + 2, nx - 1))
        states(jnp.minimum(x + 3, nx - 1))
        div = vertical(w)
        g = radial(x)
        for f in range(FIELDS):
            div[f] = div[f] + (g_ref[f] - g[f]) + along[f]
            g_ref[f] = g[f]
        finish(x, w, div)
        return 0

    lax.fori_loop(0, nx, body, 0)
    for copy in copies:
        copy.wait()

    def add(x, _):
        for f in range(FIELDS):
            acc_ref[f, x] = acc_ref[f, x] + 0.5 * old_t[f, x]
        return 0

    lax.fori_loop(0, nx, add, 0)


def outer_kernel(
    nx, wt_ref, acc_ref, ex_ref, c_ref, y_ref, xa_ref, xb_ref, out_ref, new_ref, q_ref, d_ref, sem
):
    odd_x, odd_y = lax.rem(lax.axis_index("gx"), 2), lax.rem(lax.axis_index("gy"), 2)
    lane = lanes()
    scale = 0.25 * time_step

    def ghosts(i):
        above = (odd_x == 1) != (i < 2)
        return [jnp.where(above, xb_ref[f, i % 2], xa_ref[f, i % 2]) for f in range(FIELDS)]

    def radial(w0, w1, w2, w3):
        left, right = [], []
        for f in range(FIELDS):
            mid = w2[f] - w1[f]
            left.append(w1[f] + half_slope(w1[f] - w0[f], mid))
            right.append(w2[f] - half_slope(mid, w3[f] - w2[f]))
        return twice_face(left, right, 0)

    place = lax.rem(lane, EDGE)
    low = place < 4
    for v in range(nx // ROWS):
        left, right = [], []
        for f in range(FIELDS):
            own, core, cross = ex_ref[f, v], c_ref[f, v], y_ref[f, v]
            before = jnp.where(odd_y == 1, core, cross)
            after = jnp.where(odd_y == 1, cross, core)
            end = jnp.where(low, own, after)
            start = jnp.where(low, before, own)
            w0 = jnp.where(low, pltpu.roll(end, 1, 1), pltpu.roll(start, 2, 1))
            w1 = jnp.where(low, end, pltpu.roll(start, 1, 1))
            w2 = jnp.where(low, pltpu.roll(end, 127, 1), start)
            w3 = jnp.where(low, pltpu.roll(end, 126, 1), pltpu.roll(start, 127, 1))
            mid = w2 - w1
            left.append(w1 + half_slope(w1 - w0, mid))
            right.append(w2 - half_slope(mid, w3 - w2))
        g = twice_face(left, right, 1)
        for f in range(FIELDS):
            lower = jnp.where(low, jnp.where(place == 3, pltpu.roll(g[f], 1, 1), 0.0), g[f])
            upper = jnp.where(low, g[f], jnp.where(place == 4, pltpu.roll(g[f], 127, 1), 0.0))
            q_ref[f, v] = scale * (lower - upper)

    def rows(x):
        return rows_of(wt_ref, x)

    g0 = radial(ghosts(0), ghosts(1), rows(0), rows(1))
    g1 = radial(ghosts(1), rows(0), rows(1), rows(2))
    for f in range(FIELDS):
        d_ref[f, 0] = scale * (g0[f] - g1[f])
        d_ref[f, 1] = scale * g1[f]
    g0 = radial(rows(nx - 3), rows(nx - 2), rows(nx - 1), ghosts(2))
    g1 = radial(rows(nx - 2), rows(nx - 1), ghosts(2), ghosts(3))
    for f in range(FIELDS):
        d_ref[f, 2] = -scale * g0[f]
        d_ref[f, 3] = scale * (g0[f] - g1[f])

    edge = (lane < 2) | (lane > 125)
    copies = []
    for f in range(FIELDS):
        for x in range(nx):
            q = pltpu.roll(q_ref[f, x // ROWS], (124 - EDGE * (x % ROWS)) % 128, 1)
            new = acc_ref[f, x] + jnp.where(edge, q, 0.0)
            at = {0: 0, 1: 1, nx - 2: 2, nx - 1: 3}.get(x)
            new_ref[f, x] = new if at is None else new + d_ref[f, at]
        for z in range(8):
            copy = pltpu.make_async_copy(new_ref.at[f, :, z], out_ref.at[f, z], sem.at[f, z])
            copy.start()
            copies.append(copy)
    for copy in copies:
        copy.wait()


def swaps(nx, ny):
    def at(g, j):
        return (g % nx) * ny + j % ny

    grid = [(g, j) for g in range(nx) for j in range(ny)]
    core = [(at(g, j), at(g, j ^ 1)) for g, j in grid]
    cross = [(at(g, j), at(g, j + 1 if j % 2 else j - 1)) for g, j in grid]
    along = [(at(g, j), at(g ^ 1, j)) for g, j in grid]

    def ends(k):
        there = [(at(0, j), at(nx - 1, j + k)) for j in range(ny)]
        return there + [(b, a) for a, b in there]

    def other(k):
        inside = [(at(g, j), at(g + 1 if g % 2 else g - 1, j)) for g, j in grid if 0 < g < nx - 1]
        return inside + ends(k)

    return core, cross, along, other


def on_device(old_state, section_prims, shear_whole, shear_frac):
    n_gx, n_gy = lax.axis_size("gx"), lax.axis_size("gy")
    gx, gy = lax.axis_index("gx"), lax.axis_index("gy")
    fields, nz, nx, cells = section_prims.shape
    assert (fields, nz, cells) == (FIELDS, 8, 128)
    assert nx % ROWS == 0 and n_gx % 2 == 0 and n_gy % 2 == 0
    axes = ("gx", "gy")
    core, cross, along, other = swaps(n_gx, n_gy)
    f32 = jnp.float32
    vmem = pl.BlockSpec(memory_space=pltpu.VMEM)
    smem = pl.BlockSpec(memory_space=pltpu.SMEM)
    hbm = pl.BlockSpec(memory_space=pltpu.HBM)
    block = (fields, nx, nz, cells)
    tile = (fields, nz, cells)
    tiles = nx // ROWS
    edge_rows = jax.ShapeDtypeStruct((fields, 2, nz, cells), f32)

    def room(mib):
        return pltpu.CompilerParams(vmem_limit_bytes=mib << 20)

    in_hbm = [pltpu.with_memory_space_constraint(v, pltpu.HBM) for v in (section_prims, old_state)]
    in_hbm = [shear_whole, shear_frac] + in_hbm
    wt, xa, ex, k, shift, frac = pl.pallas_call(
        functools.partial(pack_kernel, nx),
        out_shape=(
            jax.ShapeDtypeStruct(block, f32),
            edge_rows,
            jax.ShapeDtypeStruct((fields, tiles + 2, nz, cells), f32),
            jax.ShapeDtypeStruct((1,), jnp.int32),
            jax.ShapeDtypeStruct((1,), jnp.int32),
            jax.ShapeDtypeStruct((1,), f32),
        ),
        in_specs=[hbm] * 3,
        out_specs=(vmem, vmem, vmem, smem, smem, smem),
        scratch_shapes=[
            pltpu.SMEM((1,), jnp.int32),
            pltpu.SMEM((1,), f32),
            pltpu.SemaphoreType.DMA((nz,)),
            pltpu.SemaphoreType.DMA((2,)),
        ],
        compiler_params=room(8),
        name="pack",
    )(*in_hbm[:3])

    c_in = lax.ppermute(ex, axes, core)
    y_in = lax.ppermute(ex, axes, cross)
    xa_in = lax.ppermute(xa, axes, along)
    xb = pl.pallas_call(
        functools.partial(shear_kernel, nx),
        out_shape=edge_rows,
        in_specs=[smem, smem, vmem, vmem, vmem],
        out_specs=vmem,
        compiler_params=room(8),
        name="shear",
    )(shift, frac, ex, c_in, y_in)

    def branch(k):
        def run(xb, wt, old):
            xb_in = lax.ppermute(xb, axes, other(k))
            acc = pl.pallas_call(
                functools.partial(inner_kernel, nx),
                out_shape=jax.ShapeDtypeStruct(block, f32),
                in_specs=[vmem, hbm],
                out_specs=vmem,
                scratch_shapes=[pltpu.VMEM(block, f32)]
                + [pltpu.VMEM(tile, f32)] * 3
                + [pltpu.VMEM(block, f32)] * 4
                + [pltpu.SemaphoreType.DMA((nz,))],
                compiler_params=room(16),
                cost_estimate=pl.CostEstimate(
                    flops=720 * nx * nz * cells, bytes_accessed=12 * fields * nx * nz * cells, transcendentals=0
                ),
                name="inner",
            )(wt, old)
            return xb_in, acc

        return run

    xb_in, acc = lax.switch(k[0], [branch(k) for k in range(n_gy)], xb, wt, in_hbm[3])

    return pl.pallas_call(
        functools.partial(outer_kernel, nx),
        out_shape=jax.ShapeDtypeStruct(section_prims.shape, f32),
        in_specs=[vmem] * 7,
        out_specs=hbm,
        scratch_shapes=[
            pltpu.VMEM(block, f32),
            pltpu.VMEM((fields, tiles, nz, cells), f32),
            pltpu.VMEM((fields, 4, nz, cells), f32),
            pltpu.SemaphoreType.DMA((fields, nz)),
        ],
        compiler_params=room(12),
        name="outer",
    )(wt, acc, ex, c_in, y_in, xa_in, xb_in)


def solution(mesh):
    in_specs = (P(None, None, "gx", "gy"), P(None, None, "gx", "gy"), P(), P())
    out_specs = P(None, None, "gx", "gy")
    return jax.shard_map(
        on_device, mesh=mesh, in_specs=in_specs, out_specs=out_specs, check_vma=False
    )
```

```python
import functools

import jax
import jax.numpy as jnp
from jax import lax
from jax.experimental import pallas as pl
from jax.experimental.pallas import tpu as pltpu
from jax.sharding import PartitionSpec as P

gamma_gas = 5.0 / 3.0
omega_rate = 1.0
shear_rate = 1.5
time_step = 0.1

FIELDS = 8
EDGE = 8
ROWS = 128 // EDGE


def median0(a, b):
    return jnp.maximum(jnp.minimum(a, b), jnp.minimum(jnp.maximum(a, b), 0.0))


def half_slope(a, b):
    return 0.5 * median0(a, b)


def side(w, n):
    t, u = (n + 1) % 3, (n + 2) % 3
    rho, p = w[0], w[4]
    vn, vt, vu = w[1 + n], w[1 + t], w[1 + u]
    bn, bt, bu = w[5 + n], w[5 + t], w[5 + u]
    mn, mt, mu = rho * vn, rho * vt, rho * vu
    mnvn = mn * vn
    bn2 = bn * bn
    bt2 = bt * bt + bu * bu
    bsq = bn2 + bt2
    q = 0.5 * (mnvn + mt * vt + mu * vu) + p * (1.0 / (gamma_gas - 1.0))
    pm = 0.5 * bsq
    cons = [None] * FIELDS
    flux = [None] * FIELDS
    cons[0], cons[1 + n], cons[1 + t], cons[1 + u] = rho, mn, mt, mu
    cons[4] = q + pm
    cons[5 + n], cons[5 + t], cons[5 + u] = bn, bt, bu
    flux[0] = mn
    flux[1 + n] = mnvn + (p + pm - bn2)
    flux[1 + t] = mt * vn - bt * bn
    flux[1 + u] = mu * vn - bu * bn
    flux[4] = (q + p + bt2) * vn - bn * (vt * bt + vu * bu)
    flux[5 + t] = bt * vn - vt * bn
    flux[5 + u] = bu * vn - vu * bn
    a = (0.5 * gamma_gas) * p
    diff = a - pm
    disc = diff * diff + a * (bt2 + bt2)
    x = a + pm + disc * lax.rsqrt(jnp.maximum(disc, 1e-30))
    speed = jnp.abs(vn) + x * lax.rsqrt(rho * x)
    return cons, flux, speed


def twice_face(left, right, n):
    cl, fl, sl = side(left, n)
    cr, fr, sr = side(right, n)
    s = jnp.maximum(sl, sr)
    out = []
    for j in range(FIELDS):
        jump = s * (cr[j] - cl[j])
        out.append(-jump if j == 5 + n else fl[j] + fr[j] - jump)
    return out


def lanes():
    return lax.broadcasted_iota(jnp.int32, (8, 128), 1)


def rows_of(ref, x):
    return [ref[f, x] for f in range(FIELDS)]


def transposing(src, dst, sem):
    return [
        [pltpu.make_async_copy(src.at[f, z], dst.at[f, :, z], sem.at[f, z]) for z in range(8)]
        for f in range(FIELDS)
    ]


def pack_kernel(nx, w_ref, wt_ref, xa_ref, own_ref, ex_ref, sem):
    copies = transposing(w_ref, wt_ref, sem)
    for field in copies:
        for copy in field:
            copy.start()
    odd = lax.rem(lax.axis_index("gx"), 2)
    first_a = (1 - odd) * (nx - 2)
    first_b = odd * (nx - 2)
    lane = lanes()
    group, place = lane // EDGE, lax.rem(lane, EDGE)
    middle = (place > 1) & (place < 6)
    for f in range(FIELDS):
        for copy in copies[f]:
            copy.wait()
        for g in range(2):
            xa_ref[f, g] = wt_ref[f, first_a + g]
            ex_ref[f, g] = wt_ref[f, first_b + g]
        tiles = []
        for v in range(nx // ROWS):
            acc = jnp.zeros((8, 128), jnp.float32)
            for i in range(ROWS):
                row = wt_ref[f, v * ROWS + i]
                acc = jnp.where(group == i, pltpu.roll(row, (EDGE * i + 4) % 128, 1), acc)
            own_ref[f, v] = acc
            tiles.append(acc)
        for v in range(0, len(tiles), 2):
            ex_ref[f, 2 + v // 2] = jnp.where(middle, tiles[v], pltpu.roll(tiles[v + 1], 4, 1))


def shear_kernel(whole_ref, frac_ref, ex_ref, c_ref, y_ref, xb_ref):
    gx, odd_y = lax.axis_index("gx"), lax.rem(lax.axis_index("gy"), 2)
    upper = gx == lax.axis_size("gx") - 1
    end = upper | (gx == 0)
    shift = jnp.where(end, lax.rem(whole_ref[0], 128), 0)
    frac = jnp.where(end, frac_ref[0], 0.0)
    sibling = (odd_y == 1) != upper
    lane = lanes()

    def window(own, other, s):
        amount = jnp.where(upper, lax.rem(128 - s, 128), lax.rem(s, 128))
        low = jnp.where(upper, 0, s)
        high = jnp.where(upper, 128 - s, 128)
        near = (lane >= low) & (lane < high)
        return pltpu.roll(own, amount, 1), pltpu.roll(other, amount, 1), near

    for f in range(FIELDS):
        for g in range(2):
            own = ex_ref[f, g]
            other = jnp.where(sibling, c_ref[f, g], y_ref[f, g])
            a, b, near = window(own, other, shift)
            first = jnp.where(near, a, b)
            a, b, near = window(own, other, shift + 1)
            second = jnp.where(near, a, b)
            xb_ref[f, g] = (1.0 - frac) * first + frac * second


def inner_kernel(
    nx, wt_ref, old_ref, acc_ref, old_t, g_ref, l_ref, d_ref, al_ref, am_ref, ar_ref, ag_ref, sem
):
    copies = [copy for field in transposing(old_ref, old_t, sem) for copy in field]
    for copy in copies:
        copy.start()
    lane = lanes()
    whole = (lane > 0) & (lane < 126)

    def finish(x, w, div):
        rho, vx, vy, vz, p, bx, by, bz = w
        mx, my, mz = rho * vx, rho * vy, rho * vz
        energy = (
            p * (1.0 / (gamma_gas - 1.0))
            + 0.5 * (mx * vx + my * vy + mz * vz)
            + 0.5 * (bx * bx + by * by + bz * bz)
        )
        cons = [rho, mx, my, mz, energy, bx, by, bz]
        src = [None] * FIELDS
        src[1] = (time_step * 2.0 * omega_rate) * my
        src[2] = (-time_step * (2.0 - shear_rate) * omega_rate) * mx
        src[4] = (time_step * shear_rate * omega_rate) * (mx * vy - bx * by)
        src[6] = (-time_step * shear_rate * omega_rate) * bx
        for f in range(FIELDS):
            total = cons[f] + (0.5 * time_step) * div[f]
            acc_ref[f, x] = total if src[f] is None else total + src[f]

    def vertical(w):
        left, right = [], []
        for f in range(FIELDS):
            up = pltpu.roll(w[f], 7, 0) - w[f]
            h = half_slope(pltpu.roll(up, 1, 0), up)
            left.append(w[f] + h)
            right.append(pltpu.roll(w[f] - h, 7, 0))
        g = twice_face(left, right, 2)
        return [pltpu.roll(v, 1, 0) - v for v in g]

    def radial(x):
        w2 = rows_of(wt_ref, jnp.minimum(x + 1, nx - 1))
        w3 = rows_of(wt_ref, jnp.minimum(x + 2, nx - 1))
        left, right = [], []
        for f in range(FIELDS):
            step = w3[f] - w2[f]
            h = half_slope(d_ref[f], step)
            left.append(l_ref[f])
            right.append(w2[f] - h)
            l_ref[f] = w2[f] + h
            d_ref[f] = step
        keep = jnp.where((x > 0) & (x < nx - 2), 1.0, 0.0)
        return [keep * v for v in twice_face(left, right, 0)]

    def states(x):
        for f in range(FIELDS):
            w = wt_ref[f, x]
            h = half_slope(w - pltpu.roll(w, 1, 1), pltpu.roll(w, 127, 1) - w)
            al_ref[f, x] = w + h
            am_ref[f, x] = w - h

    def turn(x):
        for f in range(FIELDS):
            ar_ref[f, x] = pltpu.roll(am_ref[f, x], 127, 1)

    def faces(x):
        g = twice_face(rows_of(al_ref, x), rows_of(ar_ref, x), 1)
        for f in range(FIELDS):
            ag_ref[f, x] = jnp.where(whole, g[f], 0.0)

    states(0)
    states(1)
    states(2)
    turn(0)
    turn(1)
    faces(0)
    for f in range(FIELDS):
        g_ref[f] = jnp.zeros((8, 128), jnp.float32)
        l_ref[f] = wt_ref[f, 0]
        d_ref[f] = wt_ref[f, 1] - wt_ref[f, 0]

    def body(x, _):
        w = rows_of(wt_ref, x)
        along = rows_of(ag_ref, x)
        along = [pltpu.roll(v, 1, 1) - v for v in along]
        faces(jnp.minimum(x + 1, nx - 1))
        turn(jnp.minimum(x + 2, nx - 1))
        states(jnp.minimum(x + 3, nx - 1))
        div = vertical(w)
        g = radial(x)
        for f in range(FIELDS):
            div[f] = div[f] + (g_ref[f] - g[f]) + along[f]
            g_ref[f] = g[f]
        finish(x, w, div)
        return 0

    lax.fori_loop(0, nx, body, 0)
    for copy in copies:
        copy.wait()

    def add(x, _):
        for f in range(FIELDS):
            acc_ref[f, x] = 0.5 * (acc_ref[f, x] + old_t[f, x])
        return 0

    lax.fori_loop(0, nx, add, 0)


def outer_kernel(
    nx, wt_ref, acc_ref, own_ref, c_ref, y_ref, xa_ref, xb_hbm, out_ref,
    new_ref, q_ref, d_ref, xb_ref, sem, xb_sem,
):
    fetch = pltpu.make_async_copy(xb_hbm, xb_ref, xb_sem)
    fetch.start()
    odd_x, odd_y = lax.rem(lax.axis_index("gx"), 2), lax.rem(lax.axis_index("gy"), 2)
    lane = lanes()
    scale = 0.25 * time_step

    place = lax.rem(lane, EDGE)
    low = place < 4
    for v in range(nx // ROWS):
        left, right = [], []
        for f in range(FIELDS):
            own, core, cross = own_ref[f, v], c_ref[f, 2 + v // 2], y_ref[f, 2 + v // 2]
            before = jnp.where(odd_y == 1, core, cross)
            after = jnp.where(odd_y == 1, cross, core)
            if v % 2:
                before, after = pltpu.roll(before, 124, 1), pltpu.roll(after, 124, 1)
            end = jnp.where(low, own, after)
            start = jnp.where(low, before, own)
            w0 = jnp.where(low, pltpu.roll(end, 1, 1), pltpu.roll(start, 2, 1))
            w1 = jnp.where(low, end, pltpu.roll(start, 1, 1))
            w2 = jnp.where(low, pltpu.roll(end, 127, 1), start)
            w3 = jnp.where(low, pltpu.roll(end, 126, 1), pltpu.roll(start, 127, 1))
            mid = w2 - w1
            left.append(w1 + half_slope(w1 - w0, mid))
            right.append(w2 - half_slope(mid, w3 - w2))
        g = twice_face(left, right, 1)
        for f in range(FIELDS):
            lower = jnp.where(low, jnp.where(place == 3, pltpu.roll(g[f], 1, 1), 0.0), g[f])
            upper = jnp.where(low, g[f], jnp.where(place == 4, pltpu.roll(g[f], 127, 1), 0.0))
            q_ref[f, v] = scale * (lower - upper)

    fetch.wait()

    def ghosts(i):
        above = (odd_x == 1) != (i < 2)
        return [jnp.where(above, xb_ref[f, i % 2], xa_ref[f, i % 2]) for f in range(FIELDS)]

    def rows(x):
        return rows_of(wt_ref, x)

    def radial(w0, w1, w2, w3):
        left, right = [], []
        for f in range(FIELDS):
            mid = w2[f] - w1[f]
            left.append(w1[f] + half_slope(w1[f] - w0[f], mid))
            right.append(w2[f] - half_slope(mid, w3[f] - w2[f]))
        return twice_face(left, right, 0)

    g0 = radial(ghosts(0), ghosts(1), rows(0), rows(1))
    g1 = radial(ghosts(1), rows(0), rows(1), rows(2))
    for f in range(FIELDS):
        d_ref[f, 0] = scale * (g0[f] - g1[f])
        d_ref[f, 1] = scale * g1[f]
    g0 = radial(rows(nx - 3), rows(nx - 2), rows(nx - 1), ghosts(2))
    g1 = radial(rows(nx - 2), rows(nx - 1), ghosts(2), ghosts(3))
    for f in range(FIELDS):
        d_ref[f, 2] = -scale * g0[f]
        d_ref[f, 3] = scale * (g0[f] - g1[f])

    edge = (lane < 2) | (lane > 125)
    copies = []
    for f in range(FIELDS):
        for x in range(nx):
            q = pltpu.roll(q_ref[f, x // ROWS], (124 - EDGE * (x % ROWS)) % 128, 1)
            new = acc_ref[f, x] + jnp.where(edge, q, 0.0)
            at = {0: 0, 1: 1, nx - 2: 2, nx - 1: 3}.get(x)
            new_ref[f, x] = new if at is None else new + d_ref[f, at]
        for z in range(8):
            copy = pltpu.make_async_copy(new_ref.at[f, :, z], out_ref.at[f, z], sem.at[f, z])
            copy.start()
            copies.append(copy)
    for copy in copies:
        copy.wait()


def swaps(nx, ny):
    def at(g, j):
        return (g % nx) * ny + j % ny

    grid = [(g, j) for g in range(nx) for j in range(ny)]
    core = [(at(g, j), at(g, j ^ 1)) for g, j in grid]
    cross = [(at(g, j), at(g, j + 1 if j % 2 else j - 1)) for g, j in grid]
    along = [(at(g, j), at(g ^ 1, j)) for g, j in grid]

    def ends(k):
        there = [(at(0, j), at(nx - 1, j + k)) for j in range(ny)]
        return there + [(b, a) for a, b in there]

    def other(k):
        inside = [(at(g, j), at(g + 1 if g % 2 else g - 1, j)) for g, j in grid if 0 < g < nx - 1]
        return inside + ends(k)

    return core, cross, along, other


def on_device(old_state, section_prims, shear_whole, shear_frac):
    n_gx, n_gy = lax.axis_size("gx"), lax.axis_size("gy")
    gx, gy = lax.axis_index("gx"), lax.axis_index("gy")
    fields, nz, nx, cells = section_prims.shape
    assert (fields, nz, cells) == (FIELDS, 8, 128)
    assert nx % (2 * ROWS) == 0 and n_gx % 2 == 0 and n_gy % 2 == 0
    axes = ("gx", "gy")
    core, cross, along, other = swaps(n_gx, n_gy)
    f32 = jnp.float32
    vmem = pl.BlockSpec(memory_space=pltpu.VMEM)
    smem = pl.BlockSpec(memory_space=pltpu.SMEM)
    hbm = pl.BlockSpec(memory_space=pltpu.HBM)
    block = (fields, nx, nz, cells)
    tile = (fields, nz, cells)
    tiles = nx // ROWS
    edge_rows = jax.ShapeDtypeStruct((fields, 2, nz, cells), f32)

    def room(mib):
        return pltpu.CompilerParams(vmem_limit_bytes=mib << 20)

    w, old = (pltpu.with_memory_space_constraint(v, pltpu.HBM) for v in (section_prims, old_state))
    wt, xa, own, ex = pl.pallas_call(
        functools.partial(pack_kernel, nx),
        out_shape=(
            jax.ShapeDtypeStruct(block, f32),
            edge_rows,
            jax.ShapeDtypeStruct((fields, tiles, nz, cells), f32),
            jax.ShapeDtypeStruct((fields, 2 + tiles // 2, nz, cells), f32),
        ),
        in_specs=[hbm],
        out_specs=(vmem,) * 4,
        scratch_shapes=[pltpu.SemaphoreType.DMA((fields, nz))],
        compiler_params=room(8),
        name="pack",
    )(w)

    c_in = lax.ppermute(ex, axes, core)
    y_in = lax.ppermute(ex, axes, cross)
    xa_in = lax.ppermute(xa, axes, along)
    xb = pl.pallas_call(
        shear_kernel,
        out_shape=edge_rows,
        in_specs=[smem, smem, vmem, vmem, vmem],
        out_specs=vmem,
        compiler_params=room(8),
        name="shear",
    )(shear_whole, shear_frac, ex, c_in, y_in)

    def branch(k):
        def run(xb, wt, old):
            xb_in = lax.ppermute(xb, axes, other(k))
            acc = pl.pallas_call(
                functools.partial(inner_kernel, nx),
                out_shape=jax.ShapeDtypeStruct(block, f32),
                in_specs=[vmem, hbm],
                out_specs=vmem,
                scratch_shapes=[pltpu.VMEM(block, f32)]
                + [pltpu.VMEM(tile, f32)] * 3
                + [pltpu.VMEM(block, f32)] * 4
                + [pltpu.SemaphoreType.DMA((fields, nz))],
                compiler_params=room(16),
                cost_estimate=pl.CostEstimate(
                    flops=720 * nx * nz * cells, bytes_accessed=12 * fields * nx * nz * cells, transcendentals=0
                ),
                name="inner",
            )(wt, old)
            return xb_in, acc

        return run

    whole = lax.shift_right_logical(shear_whole[0], 7)
    xb_in, acc = lax.switch(whole, [branch(k) for k in range(n_gy)], xb, wt, old)

    return pl.pallas_call(
        functools.partial(outer_kernel, nx),
        out_shape=jax.ShapeDtypeStruct(section_prims.shape, f32),
        in_specs=[vmem] * 6 + [hbm],
        out_specs=hbm,
        scratch_shapes=[
            pltpu.VMEM(block, f32),
            pltpu.VMEM((fields, tiles, nz, cells), f32),
            pltpu.VMEM((fields, 4, nz, cells), f32),
            pltpu.VMEM((fields, 2, nz, cells), f32),
            pltpu.SemaphoreType.DMA((fields, nz)),
            pltpu.SemaphoreType.DMA,
        ],
        compiler_params=room(12),
        name="outer",
    )(wt, acc, own, c_in, y_in, xa_in, xb_in)


def solution(mesh):
    in_specs = (P(None, None, "gx", "gy"), P(None, None, "gx", "gy"), P(), P())
    out_specs = P(None, None, "gx", "gy")
    return jax.shard_map(
        on_device, mesh=mesh, in_specs=in_specs, out_specs=out_specs, check_vma=False
    )
```

```python
import functools

import jax
import jax.numpy as jnp
from jax import lax
from jax.experimental import pallas as pl
from jax.experimental.pallas import tpu as pltpu
from jax.sharding import PartitionSpec as P

gamma_gas = 5.0 / 3.0
omega_rate = 1.0
shear_rate = 1.5
time_step = 0.1

FIELDS = 8
EDGE = 8
ROWS = 128 // EDGE
UNROLL = 2


def median0(a, b):
    return jnp.maximum(jnp.minimum(a, b), jnp.minimum(jnp.maximum(a, b), 0.0))


def half_slope(a, b):
    return 0.5 * median0(a, b)


def side(w, n):
    t, u = (n + 1) % 3, (n + 2) % 3
    rho, p = w[0], w[4]
    vn, vt, vu = w[1 + n], w[1 + t], w[1 + u]
    bn, bt, bu = w[5 + n], w[5 + t], w[5 + u]
    mn, mt, mu = rho * vn, rho * vt, rho * vu
    mnvn = mn * vn
    bn2 = bn * bn
    bt2 = bt * bt + bu * bu
    bsq = bn2 + bt2
    q = 0.5 * (mnvn + mt * vt + mu * vu) + p * (1.0 / (gamma_gas - 1.0))
    pm = 0.5 * bsq
    cons = [None] * FIELDS
    flux = [None] * FIELDS
    cons[0], cons[1 + n], cons[1 + t], cons[1 + u] = rho, mn, mt, mu
    cons[4] = q + pm
    cons[5 + n], cons[5 + t], cons[5 + u] = bn, bt, bu
    flux[0] = mn
    flux[1 + n] = mnvn + (p + pm - bn2)
    flux[1 + t] = mt * vn - bt * bn
    flux[1 + u] = mu * vn - bu * bn
    flux[4] = (q + p + bt2) * vn - bn * (vt * bt + vu * bu)
    flux[5 + t] = bt * vn - vt * bn
    flux[5 + u] = bu * vn - vu * bn
    a = (0.5 * gamma_gas) * p
    diff = a - pm
    disc = diff * diff + a * (bt2 + bt2)
    x = a + pm + disc * lax.rsqrt(jnp.maximum(disc, 1e-30))
    speed = jnp.abs(vn) + x * lax.rsqrt(rho * x)
    return cons, flux, speed


def twice_face(left, right, n):
    cl, fl, sl = side(left, n)
    cr, fr, sr = side(right, n)
    s = jnp.maximum(sl, sr)
    out = []
    for j in range(FIELDS):
        jump = s * (cr[j] - cl[j])
        out.append(-jump if j == 5 + n else fl[j] + fr[j] - jump)
    return out


def lanes():
    return lax.broadcasted_iota(jnp.int32, (8, 128), 1)


def rows_of(ref, x):
    return [ref[f, x] for f in range(FIELDS)]


def transposing(src, dst, sem, parts):
    n = FIELDS // parts
    return [
        [
            pltpu.make_async_copy(
                src.at[n * i : n * i + n, z], dst.at[n * i : n * i + n, :, z], sem.at[i, z]
            )
            for z in range(8)
        ]
        for i in range(parts)
    ]


def upright(nx, wt_ref, acc_ref):
    def body(x, _):
        w = rows_of(wt_ref, x)
        left, right = [], []
        for f in range(FIELDS):
            up = pltpu.roll(w[f], 7, 0) - w[f]
            h = half_slope(pltpu.roll(up, 1, 0), up)
            left.append(w[f] + h)
            right.append(pltpu.roll(w[f] - h, 7, 0))
        g = twice_face(left, right, 2)
        rho, vx, vy, vz, p, bx, by, bz = w
        mx, my, mz = rho * vx, rho * vy, rho * vz
        energy = (
            p * (1.0 / (gamma_gas - 1.0))
            + 0.5 * (mx * vx + my * vy + mz * vz)
            + 0.5 * (bx * bx + by * by + bz * bz)
        )
        cons = [rho, mx, my, mz, energy, bx, by, bz]
        src = [None] * FIELDS
        src[1] = (time_step * 2.0 * omega_rate) * my
        src[2] = (-time_step * (2.0 - shear_rate) * omega_rate) * mx
        src[4] = (time_step * shear_rate * omega_rate) * (mx * vy - bx * by)
        src[6] = (-time_step * shear_rate * omega_rate) * bx
        for f in range(FIELDS):
            total = cons[f] + (0.5 * time_step) * (pltpu.roll(g[f], 1, 0) - g[f])
            acc_ref[f, x] = total if src[f] is None else total + src[f]
        return 0

    lax.fori_loop(0, nx, body, 0)


def early():
    return lax.axis_index("gy") == 0


def upright_kernel(nx, wt_ref, acc_in, acc_ref):
    @pl.when(jnp.logical_not(early()))
    def _():
        upright(nx, wt_ref, acc_ref)


def pack_kernel(nx, w_ref, wt_ref, xa_ref, own_ref, ex_ref, acc_ref, sem):
    parts = sem.shape[0]
    copies = transposing(w_ref, wt_ref, sem, parts)
    for part in copies:
        for copy in part:
            copy.start()
    odd = lax.rem(lax.axis_index("gx"), 2)
    first_a = (1 - odd) * (nx - 2)
    first_b = odd * (nx - 2)
    lane = lanes()
    group, place = lane // EDGE, lax.rem(lane, EDGE)
    middle = (place > 1) & (place < 6)
    for f in range(FIELDS):
        if f % (FIELDS // parts) == 0:
            for copy in copies[f // (FIELDS // parts)]:
                copy.wait()
        for g in range(2):
            xa_ref[f, g] = wt_ref[f, first_a + g]
            ex_ref[f, g] = wt_ref[f, first_b + g]
        tiles = []
        for v in range(nx // ROWS):
            acc = jnp.zeros((8, 128), jnp.float32)
            for i in range(ROWS):
                row = wt_ref[f, v * ROWS + i]
                acc = jnp.where(group == i, pltpu.roll(row, (EDGE * i + 4) % 128, 1), acc)
            own_ref[f, v] = acc
            tiles.append(acc)
        for v in range(0, len(tiles), 2):
            ex_ref[f, 2 + v // 2] = jnp.where(middle, tiles[v], pltpu.roll(tiles[v + 1], 4, 1))

    @pl.when(early())
    def _():
        upright(nx, wt_ref, acc_ref)


def shear_kernel(whole_ref, frac_ref, ex_ref, c_ref, y_ref, acc_ref, xb_ref):
    gx, odd_y = lax.axis_index("gx"), lax.rem(lax.axis_index("gy"), 2)
    upper = gx == lax.axis_size("gx") - 1
    end = upper | (gx == 0)
    shift = jnp.where(end, lax.rem(whole_ref[0], 128), 0)
    frac = jnp.where(end, frac_ref[0], 0.0)
    sibling = (odd_y == 1) != upper
    lane = lanes()

    def window(own, other, s):
        amount = jnp.where(upper, lax.rem(128 - s, 128), lax.rem(s, 128))
        low = jnp.where(upper, 0, s)
        high = jnp.where(upper, 128 - s, 128)
        near = (lane >= low) & (lane < high)
        return pltpu.roll(own, amount, 1), pltpu.roll(other, amount, 1), near

    for f in range(FIELDS):
        for g in range(2):
            own = ex_ref[f, g]
            other = jnp.where(sibling, c_ref[f, g], y_ref[f, g])
            a, b, near = window(own, other, shift)
            first = jnp.where(near, a, b)
            a, b, near = window(own, other, shift + 1)
            second = jnp.where(near, a, b)
            xb_ref[f, g] = (1.0 - frac) * first + frac * second


def inner_kernel(
    nx, wt_ref, up_ref, old_ref, acc_ref, old_t, g_ref, l_ref, d_ref, al_ref, am_ref, ar_ref, ag_ref, sem
):
    copies = transposing(old_ref, old_t, sem, 1)[0]
    for copy in copies:
        copy.start()
    lane = lanes()
    whole = (lane > 0) & (lane < 126)

    def radial(x, l, d):
        w2 = rows_of(wt_ref, jnp.minimum(x + 1, nx - 1))
        w3 = rows_of(wt_ref, jnp.minimum(x + 2, nx - 1))
        right, next_l, next_d = [], [], []
        for f in range(FIELDS):
            step = w3[f] - w2[f]
            h = half_slope(d[f], step)
            right.append(w2[f] - h)
            next_l.append(w2[f] + h)
            next_d.append(step)
        keep = jnp.where((x > 0) & (x < nx - 2), 1.0, 0.0)
        return [keep * v for v in twice_face(l, right, 0)], next_l, next_d

    def states(x):
        for f in range(FIELDS):
            w = wt_ref[f, x]
            h = half_slope(w - pltpu.roll(w, 1, 1), pltpu.roll(w, 127, 1) - w)
            al_ref[f, x] = w + h
            am_ref[f, x] = w - h

    def turn(x):
        for f in range(FIELDS):
            ar_ref[f, x] = pltpu.roll(am_ref[f, x], 127, 1)

    def faces(x):
        g = twice_face(rows_of(al_ref, x), rows_of(ar_ref, x), 1)
        for f in range(FIELDS):
            ag_ref[f, x] = jnp.where(whole, g[f], 0.0)

    for i in range(3 * UNROLL):
        states(i)
    for i in range(2 * UNROLL):
        turn(i)
    for i in range(UNROLL):
        faces(i)
    for f in range(FIELDS):
        g_ref[f] = jnp.zeros((8, 128), jnp.float32)
        l_ref[f] = wt_ref[f, 0]
        d_ref[f] = wt_ref[f, 1] - wt_ref[f, 0]

    def body(i, _):
        first = i * UNROLL
        rows = [first + j for j in range(UNROLL)]
        along = [[pltpu.roll(v, 1, 1) - v for v in rows_of(ag_ref, x)] for x in rows]
        for stage, ahead in ((faces, 1), (turn, 2), (states, 3)):
            for x in rows:
                stage(jnp.minimum(x + ahead * UNROLL, nx - 1))
        l, d, below = ([ref[f] for f in range(FIELDS)] for ref in (l_ref, d_ref, g_ref))
        for x, turned in zip(rows, along):
            g, l, d = radial(x, l, d)
            for f in range(FIELDS):
                div = (below[f] - g[f]) + turned[f]
                acc_ref[f, x] = up_ref[f, x] + (0.5 * time_step) * div
            below = g
        for f in range(FIELDS):
            l_ref[f], d_ref[f], g_ref[f] = l[f], d[f], below[f]
        return 0

    lax.fori_loop(0, nx // UNROLL, body, 0)
    for copy in copies:
        copy.wait()


def outer_kernel(
    nx, wt_ref, acc_ref, old_ref, own_ref, c_ref, y_ref, xa_ref, xb_hbm, out_ref,
    new_ref, q_ref, d_ref, xb_ref, sem, xb_sem,
):
    fetch = pltpu.make_async_copy(xb_hbm, xb_ref, xb_sem)
    fetch.start()
    odd_x, odd_y = lax.rem(lax.axis_index("gx"), 2), lax.rem(lax.axis_index("gy"), 2)
    lane = lanes()
    scale = 0.25 * time_step

    place = lax.rem(lane, EDGE)
    low = place < 4
    for v in range(nx // ROWS):
        left, right = [], []
        for f in range(FIELDS):
            own, core, cross = own_ref[f, v], c_ref[f, 2 + v // 2], y_ref[f, 2 + v // 2]
            before = jnp.where(odd_y == 1, core, cross)
            after = jnp.where(odd_y == 1, cross, core)
            if v % 2:
                before, after = pltpu.roll(before, 124, 1), pltpu.roll(after, 124, 1)
            end = jnp.where(low, own, after)
            start = jnp.where(low, before, own)
            w0 = jnp.where(low, pltpu.roll(end, 1, 1), pltpu.roll(start, 2, 1))
            w1 = jnp.where(low, end, pltpu.roll(start, 1, 1))
            w2 = jnp.where(low, pltpu.roll(end, 127, 1), start)
            w3 = jnp.where(low, pltpu.roll(end, 126, 1), pltpu.roll(start, 127, 1))
            mid = w2 - w1
            left.append(w1 + half_slope(w1 - w0, mid))
            right.append(w2 - half_slope(mid, w3 - w2))
        g = twice_face(left, right, 1)
        for f in range(FIELDS):
            lower = jnp.where(low, jnp.where(place == 3, pltpu.roll(g[f], 1, 1), 0.0), g[f])
            upper = jnp.where(low, g[f], jnp.where(place == 4, pltpu.roll(g[f], 127, 1), 0.0))
            q_ref[f, v] = scale * (lower - upper)

    fetch.wait()

    def ghosts(i):
        above = (odd_x == 1) != (i < 2)
        return [jnp.where(above, xb_ref[f, i % 2], xa_ref[f, i % 2]) for f in range(FIELDS)]

    def rows(x):
        return rows_of(wt_ref, x)

    def radial(w0, w1, w2, w3):
        left, right = [], []
        for f in range(FIELDS):
            mid = w2[f] - w1[f]
            left.append(w1[f] + half_slope(w1[f] - w0[f], mid))
            right.append(w2[f] - half_slope(mid, w3[f] - w2[f]))
        return twice_face(left, right, 0)

    g0 = radial(ghosts(0), ghosts(1), rows(0), rows(1))
    g1 = radial(ghosts(1), rows(0), rows(1), rows(2))
    for f in range(FIELDS):
        d_ref[f, 0] = scale * (g0[f] - g1[f])
        d_ref[f, 1] = scale * g1[f]
    g0 = radial(rows(nx - 3), rows(nx - 2), rows(nx - 1), ghosts(2))
    g1 = radial(rows(nx - 2), rows(nx - 1), ghosts(2), ghosts(3))
    for f in range(FIELDS):
        d_ref[f, 2] = -scale * g0[f]
        d_ref[f, 3] = scale * (g0[f] - g1[f])

    edge = (lane < 2) | (lane > 125)
    copies = []
    for f in range(FIELDS):
        for x in range(nx):
            q = pltpu.roll(q_ref[f, x // ROWS], (124 - EDGE * (x % ROWS)) % 128, 1)
            new = 0.5 * (acc_ref[f, x] + old_ref[f, x]) + jnp.where(edge, q, 0.0)
            at = {0: 0, 1: 1, nx - 2: 2, nx - 1: 3}.get(x)
            new_ref[f, x] = new if at is None else new + d_ref[f, at]
        for z in range(8):
            copy = pltpu.make_async_copy(new_ref.at[f, :, z], out_ref.at[f, z], sem.at[f, z])
            copy.start()
            copies.append(copy)
    for copy in copies:
        copy.wait()


def swaps(nx, ny):
    def at(g, j):
        return (g % nx) * ny + j % ny

    grid = [(g, j) for g in range(nx) for j in range(ny)]
    core = [(at(g, j), at(g, j ^ 1)) for g, j in grid]
    cross = [(at(g, j), at(g, j + 1 if j % 2 else j - 1)) for g, j in grid]
    along = [(at(g, j), at(g ^ 1, j)) for g, j in grid]

    def ends(k):
        there = [(at(0, j), at(nx - 1, j + k)) for j in range(ny)]
        return there + [(b, a) for a, b in there]

    def other(k):
        inside = [(at(g, j), at(g + 1 if g % 2 else g - 1, j)) for g, j in grid if 0 < g < nx - 1]
        return inside + ends(k)

    return core, cross, along, other


def on_device(old_state, section_prims, shear_whole, shear_frac):
    n_gx, n_gy = lax.axis_size("gx"), lax.axis_size("gy")
    gx, gy = lax.axis_index("gx"), lax.axis_index("gy")
    fields, nz, nx, cells = section_prims.shape
    assert (fields, nz, cells) == (FIELDS, 8, 128)
    assert nx % (2 * ROWS) == 0 and n_gx % 2 == 0 and n_gy % 2 == 0
    axes = ("gx", "gy")
    core, cross, along, other = swaps(n_gx, n_gy)
    f32 = jnp.float32
    vmem = pl.BlockSpec(memory_space=pltpu.VMEM)
    smem = pl.BlockSpec(memory_space=pltpu.SMEM)
    hbm = pl.BlockSpec(memory_space=pltpu.HBM)
    block = (fields, nx, nz, cells)
    tile = (fields, nz, cells)
    tiles = nx // ROWS
    edge_rows = jax.ShapeDtypeStruct((fields, 2, nz, cells), f32)

    def room(mib):
        return pltpu.CompilerParams(vmem_limit_bytes=mib << 20)

    def cost(flops):
        n = nx * nz * cells
        return pl.CostEstimate(flops=flops * n, bytes_accessed=12 * fields * n, transcendentals=0)

    w, old = (pltpu.with_memory_space_constraint(v, pltpu.HBM) for v in (section_prims, old_state))
    wt, xa, own, ex, acc = pl.pallas_call(
        functools.partial(pack_kernel, nx),
        out_shape=(
            jax.ShapeDtypeStruct(block, f32),
            edge_rows,
            jax.ShapeDtypeStruct((fields, tiles, nz, cells), f32),
            jax.ShapeDtypeStruct((fields, 2 + tiles // 2, nz, cells), f32),
            jax.ShapeDtypeStruct(block, f32),
        ),
        in_specs=[hbm],
        out_specs=(vmem,) * 5,
        scratch_shapes=[pltpu.SemaphoreType.DMA((2, nz))],
        compiler_params=room(8),
        name="pack",
    )(w)

    c_in = lax.ppermute(ex, axes, core)
    y_in = lax.ppermute(ex, axes, cross)
    xa_in = lax.ppermute(xa, axes, along)
    acc = pl.pallas_call(
        functools.partial(upright_kernel, nx),
        out_shape=jax.ShapeDtypeStruct(block, f32),
        in_specs=[vmem, vmem],
        out_specs=vmem,
        input_output_aliases={1: 0},
        compiler_params=room(8),
        cost_estimate=cost(300),
        name="upright",
    )(wt, acc)
    xb = pl.pallas_call(
        shear_kernel,
        out_shape=edge_rows,
        in_specs=[smem, smem, vmem, vmem, vmem, pl.BlockSpec(memory_space=pl.ANY)],
        out_specs=vmem,
        compiler_params=room(8),
        name="shear",
    )(shear_whole, shear_frac, ex, c_in, y_in, acc)

    def branch(k):
        def run(xb, wt, acc, old):
            xb_in = lax.ppermute(xb, axes, other(k))
            acc, old_t = pl.pallas_call(
                functools.partial(inner_kernel, nx),
                out_shape=(jax.ShapeDtypeStruct(block, f32),) * 2,
                in_specs=[vmem, vmem, hbm],
                out_specs=(vmem, vmem),
                scratch_shapes=[pltpu.VMEM(tile, f32)] * 3
                + [pltpu.VMEM(block, f32)] * 4
                + [pltpu.SemaphoreType.DMA((1, nz))],
                compiler_params=room(16),
                cost_estimate=cost(480),
                name="inner",
            )(wt, acc, old)
            return xb_in, acc, old_t

        return run

    whole = lax.shift_right_logical(shear_whole[0], 7)
    xb_in, acc, old_t = lax.switch(whole, [branch(k) for k in range(n_gy)], xb, wt, acc, old)

    return pl.pallas_call(
        functools.partial(outer_kernel, nx),
        out_shape=jax.ShapeDtypeStruct(section_prims.shape, f32),
        in_specs=[vmem] * 7 + [hbm],
        out_specs=hbm,
        scratch_shapes=[
            pltpu.VMEM(block, f32),
            pltpu.VMEM((fields, tiles, nz, cells), f32),
            pltpu.VMEM((fields, 4, nz, cells), f32),
            pltpu.VMEM((fields, 2, nz, cells), f32),
            pltpu.SemaphoreType.DMA((fields, nz)),
            pltpu.SemaphoreType.DMA,
        ],
        compiler_params=room(12),
        name="outer",
    )(wt, acc, old_t, own, c_in, y_in, xa_in, xb_in)


def solution(mesh):
    in_specs = (P(None, None, "gx", "gy"), P(None, None, "gx", "gy"), P(), P())
    out_specs = P(None, None, "gx", "gy")
    return jax.shard_map(
        on_device, mesh=mesh, in_specs=in_specs, out_specs=out_specs, check_vma=False
    )
```

```python
import functools

import jax
import jax.numpy as jnp
from jax import lax
from jax.experimental import pallas as pl
from jax.experimental.pallas import tpu as pltpu
from jax.sharding import PartitionSpec as P

gamma_gas = 5.0 / 3.0
omega_rate = 1.0
shear_rate = 1.5
time_step = 0.1

FIELDS = 8
EDGE = 8
ROWS = 128 // EDGE
UNROLL = 2


def median0(a, b):
    return jnp.maximum(jnp.minimum(a, b), jnp.minimum(jnp.maximum(a, b), 0.0))


def half_slope(a, b):
    return 0.5 * median0(a, b)


def side(w, n):
    t, u = (n + 1) % 3, (n + 2) % 3
    rho, p = w[0], w[4]
    vn, vt, vu = w[1 + n], w[1 + t], w[1 + u]
    bn, bt, bu = w[5 + n], w[5 + t], w[5 + u]
    mn, mt, mu = rho * vn, rho * vt, rho * vu
    mnvn = mn * vn
    bn2 = bn * bn
    bt2 = bt * bt + bu * bu
    bsq = bn2 + bt2
    q = 0.5 * (mnvn + mt * vt + mu * vu) + p * (1.0 / (gamma_gas - 1.0))
    pm = 0.5 * bsq
    cons = [None] * FIELDS
    flux = [None] * FIELDS
    cons[0], cons[1 + n], cons[1 + t], cons[1 + u] = rho, mn, mt, mu
    cons[4] = q + pm
    cons[5 + n], cons[5 + t], cons[5 + u] = bn, bt, bu
    flux[0] = mn
    flux[1 + n] = mnvn + (p + pm - bn2)
    flux[1 + t] = mt * vn - bt * bn
    flux[1 + u] = mu * vn - bu * bn
    flux[4] = (q + p + bt2) * vn - bn * (vt * bt + vu * bu)
    flux[5 + t] = bt * vn - vt * bn
    flux[5 + u] = bu * vn - vu * bn
    a = (0.5 * gamma_gas) * p
    diff = a - pm
    disc = diff * diff + a * (bt2 + bt2)
    x = a + pm + disc * lax.rsqrt(jnp.maximum(disc, 1e-30))
    speed = jnp.abs(vn) + x * lax.rsqrt(rho * x)
    return cons, flux, speed


def twice_face(left, right, n):
    cl, fl, sl = side(left, n)
    cr, fr, sr = side(right, n)
    s = jnp.maximum(sl, sr)
    out = []
    for j in range(FIELDS):
        jump = s * (cr[j] - cl[j])
        out.append(-jump if j == 5 + n else fl[j] + fr[j] - jump)
    return out


def lanes():
    return lax.broadcasted_iota(jnp.int32, (8, 128), 1)


def rows_of(ref, x):
    return [ref[f, x] for f in range(FIELDS)]


def transposing(src, dst, sem, parts):
    n = FIELDS // parts
    return [
        [
            pltpu.make_async_copy(
                src.at[n * i : n * i + n, z], dst.at[n * i : n * i + n, :, z], sem.at[i, z]
            )
            for z in range(8)
        ]
        for i in range(parts)
    ]


def upright(nx, wt_ref, acc_ref):
    def body(x, _):
        w = rows_of(wt_ref, x)
        left, right = [], []
        for f in range(FIELDS):
            up = pltpu.roll(w[f], 7, 0) - w[f]
            h = half_slope(pltpu.roll(up, 1, 0), up)
            left.append(w[f] + h)
            right.append(pltpu.roll(w[f] - h, 7, 0))
        g = twice_face(left, right, 2)
        rho, vx, vy, vz, p, bx, by, bz = w
        mx, my, mz = rho * vx, rho * vy, rho * vz
        energy = (
            p * (1.0 / (gamma_gas - 1.0))
            + 0.5 * (mx * vx + my * vy + mz * vz)
            + 0.5 * (bx * bx + by * by + bz * bz)
        )
        cons = [rho, mx, my, mz, energy, bx, by, bz]
        src = [None] * FIELDS
        src[1] = (time_step * 2.0 * omega_rate) * my
        src[2] = (-time_step * (2.0 - shear_rate) * omega_rate) * mx
        src[4] = (time_step * shear_rate * omega_rate) * (mx * vy - bx * by)
        src[6] = (-time_step * shear_rate * omega_rate) * bx
        for f in range(FIELDS):
            total = cons[f] + (0.5 * time_step) * (pltpu.roll(g[f], 1, 0) - g[f])
            acc_ref[f, x] = total if src[f] is None else total + src[f]
        return 0

    lax.fori_loop(0, nx, body, 0)


def early():
    return (lax.axis_index("gx") == 0) & (lax.axis_index("gy") < 2)


def upright_kernel(nx, wt_ref, acc_in, acc_ref):
    @pl.when(jnp.logical_not(early()))
    def _():
        upright(nx, wt_ref, acc_ref)


def pack_kernel(nx, w_ref, wt_ref, xa_ref, own_ref, ex_ref, acc_ref, sem):
    parts = sem.shape[0]
    copies = transposing(w_ref, wt_ref, sem, parts)
    for part in copies:
        for copy in part:
            copy.start()
    odd = lax.rem(lax.axis_index("gx"), 2)
    first_a = (1 - odd) * (nx - 2)
    first_b = odd * (nx - 2)
    lane = lanes()
    group, place = lane // EDGE, lax.rem(lane, EDGE)
    middle = (place > 1) & (place < 6)
    for f in range(FIELDS):
        if f % (FIELDS // parts) == 0:
            for copy in copies[f // (FIELDS // parts)]:
                copy.wait()
        for g in range(2):
            xa_ref[f, g] = wt_ref[f, first_a + g]
            ex_ref[f, g] = wt_ref[f, first_b + g]
        tiles = []
        for v in range(nx // ROWS):
            acc = jnp.zeros((8, 128), jnp.float32)
            for i in range(ROWS):
                row = wt_ref[f, v * ROWS + i]
                acc = jnp.where(group == i, pltpu.roll(row, (EDGE * i + 4) % 128, 1), acc)
            own_ref[f, v] = acc
            tiles.append(acc)
        for v in range(0, len(tiles), 2):
            ex_ref[f, 2 + v // 2] = jnp.where(middle, tiles[v], pltpu.roll(tiles[v + 1], 4, 1))

    @pl.when(early())
    def _():
        upright(nx, wt_ref, acc_ref)


def shear_kernel(whole_ref, frac_ref, ex_ref, c_ref, y_ref, acc_ref, xb_ref):
    gx, odd_y = lax.axis_index("gx"), lax.rem(lax.axis_index("gy"), 2)
    upper = gx == lax.axis_size("gx") - 1
    end = upper | (gx == 0)
    shift = jnp.where(end, lax.rem(whole_ref[0], 128), 0)
    frac = jnp.where(end, frac_ref[0], 0.0)
    sibling = (odd_y == 1) != upper
    lane = lanes()

    def window(own, other, s):
        amount = jnp.where(upper, lax.rem(128 - s, 128), lax.rem(s, 128))
        low = jnp.where(upper, 0, s)
        high = jnp.where(upper, 128 - s, 128)
        near = (lane >= low) & (lane < high)
        return pltpu.roll(own, amount, 1), pltpu.roll(other, amount, 1), near

    for f in range(FIELDS):
        for g in range(2):
            own = ex_ref[f, g]
            other = jnp.where(sibling, c_ref[f, g], y_ref[f, g])
            a, b, near = window(own, other, shift)
            first = jnp.where(near, a, b)
            a, b, near = window(own, other, shift + 1)
            second = jnp.where(near, a, b)
            xb_ref[f, g] = (1.0 - frac) * first + frac * second


def inner_kernel(
    nx, wt_ref, up_ref, old_ref, own_ref, c_ref, y_ref, out_ref, edge_ref,
    acc_ref, old_t, new_ref, q_ref, g_ref, l_ref, d_ref, al_ref, am_ref, ar_ref, ag_ref, sem, out_sem,
):
    copies = transposing(old_ref, old_t, sem, 1)[0]
    for copy in copies:
        copy.start()
    lane = lanes()
    whole = (lane > 0) & (lane < 126)

    def radial(x, l, d):
        w2 = rows_of(wt_ref, jnp.minimum(x + 1, nx - 1))
        w3 = rows_of(wt_ref, jnp.minimum(x + 2, nx - 1))
        right, next_l, next_d = [], [], []
        for f in range(FIELDS):
            step = w3[f] - w2[f]
            h = half_slope(d[f], step)
            right.append(w2[f] - h)
            next_l.append(w2[f] + h)
            next_d.append(step)
        keep = jnp.where((x > 0) & (x < nx - 2), 1.0, 0.0)
        return [keep * v for v in twice_face(l, right, 0)], next_l, next_d

    def states(x):
        for f in range(FIELDS):
            w = wt_ref[f, x]
            h = half_slope(w - pltpu.roll(w, 1, 1), pltpu.roll(w, 127, 1) - w)
            al_ref[f, x] = w + h
            am_ref[f, x] = w - h

    def turn(x):
        for f in range(FIELDS):
            ar_ref[f, x] = pltpu.roll(am_ref[f, x], 127, 1)

    def faces(x):
        g = twice_face(rows_of(al_ref, x), rows_of(ar_ref, x), 1)
        for f in range(FIELDS):
            ag_ref[f, x] = jnp.where(whole, g[f], 0.0)

    for i in range(3 * UNROLL):
        states(i)
    for i in range(2 * UNROLL):
        turn(i)
    for i in range(UNROLL):
        faces(i)
    for f in range(FIELDS):
        g_ref[f] = jnp.zeros((8, 128), jnp.float32)
        l_ref[f] = wt_ref[f, 0]
        d_ref[f] = wt_ref[f, 1] - wt_ref[f, 0]

    def body(i, _):
        first = i * UNROLL
        rows = [first + j for j in range(UNROLL)]
        along = [[pltpu.roll(v, 1, 1) - v for v in rows_of(ag_ref, x)] for x in rows]
        for stage, ahead in ((faces, 1), (turn, 2), (states, 3)):
            for x in rows:
                stage(jnp.minimum(x + ahead * UNROLL, nx - 1))
        l, d, below = ([ref[f] for f in range(FIELDS)] for ref in (l_ref, d_ref, g_ref))
        for x, turned in zip(rows, along):
            g, l, d = radial(x, l, d)
            for f in range(FIELDS):
                div = (below[f] - g[f]) + turned[f]
                acc_ref[f, x] = up_ref[f, x] + (0.5 * time_step) * div
            below = g
        for f in range(FIELDS):
            l_ref[f], d_ref[f], g_ref[f] = l[f], d[f], below[f]
        return 0

    lax.fori_loop(0, nx // UNROLL, body, 0)
    odd_y = lax.rem(lax.axis_index("gy"), 2)
    scale = 0.25 * time_step
    place = lax.rem(lane, EDGE)
    low = place < 4
    for v in range(nx // ROWS):
        left, right = [], []
        for f in range(FIELDS):
            own, core, cross = own_ref[f, v], c_ref[f, 2 + v // 2], y_ref[f, 2 + v // 2]
            before = jnp.where(odd_y == 1, core, cross)
            after = jnp.where(odd_y == 1, cross, core)
            if v % 2:
                before, after = pltpu.roll(before, 124, 1), pltpu.roll(after, 124, 1)
            end = jnp.where(low, own, after)
            start = jnp.where(low, before, own)
            w0 = jnp.where(low, pltpu.roll(end, 1, 1), pltpu.roll(start, 2, 1))
            w1 = jnp.where(low, end, pltpu.roll(start, 1, 1))
            w2 = jnp.where(low, pltpu.roll(end, 127, 1), start)
            w3 = jnp.where(low, pltpu.roll(end, 126, 1), pltpu.roll(start, 127, 1))
            mid = w2 - w1
            left.append(w1 + half_slope(w1 - w0, mid))
            right.append(w2 - half_slope(mid, w3 - w2))
        g = twice_face(left, right, 1)
        for f in range(FIELDS):
            lower = jnp.where(low, jnp.where(place == 3, pltpu.roll(g[f], 1, 1), 0.0), g[f])
            upper = jnp.where(low, g[f], jnp.where(place == 4, pltpu.roll(g[f], 127, 1), 0.0))
            q_ref[f, v] = scale * (lower - upper)

    for copy in copies:
        copy.wait()
    ends = (lane < 2) | (lane > 125)
    parts = out_sem.shape[0]
    copies = []
    for f in range(FIELDS):
        for x in range(nx):
            q = pltpu.roll(q_ref[f, x // ROWS], (124 - EDGE * (x % ROWS)) % 128, 1)
            new = 0.5 * (acc_ref[f, x] + old_t[f, x]) + jnp.where(ends, q, 0.0)
            if x < 8:
                edge_ref[f, x] = new
            elif x >= nx - 8:
                edge_ref[f, x - nx + 16] = new
            else:
                new_ref[f, x - 8] = new
        if (f + 1) % (FIELDS // parts) == 0:
            part = (f + 1) // (FIELDS // parts) - 1
            span = slice(f + 1 - FIELDS // parts, f + 1)
            for z in range(8):
                copy = pltpu.make_async_copy(
                    new_ref.at[span, :, z], out_ref.at[span, z, 8 : nx - 8], out_sem.at[part, z]
                )
                copy.start()
                copies.append(copy)
    for copy in copies:
        copy.wait()


def outer_kernel(
    nx, wt_ref, edge_ref, xa_ref, xb_hbm, part_ref, out_ref, new_ref, xb_ref, sem, xb_sem
):
    fetch = pltpu.make_async_copy(xb_hbm, xb_ref, xb_sem)
    fetch.start()
    odd_x = lax.rem(lax.axis_index("gx"), 2)
    scale = 0.25 * time_step
    for f in range(FIELDS):
        for i in range(16):
            new_ref[f, i] = edge_ref[f, i]

    def rows(x):
        return rows_of(wt_ref, x)

    def ghosts(i):
        above = (odd_x == 1) != (i < 2)
        return [jnp.where(above, xb_ref[f, i % 2], xa_ref[f, i % 2]) for f in range(FIELDS)]

    def radial(w0, w1, w2, w3):
        left, right = [], []
        for f in range(FIELDS):
            mid = w2[f] - w1[f]
            left.append(w1[f] + half_slope(w1[f] - w0[f], mid))
            right.append(w2[f] - half_slope(mid, w3[f] - w2[f]))
        return twice_face(left, right, 0)

    def send(i):
        first = (nx - 8) * i
        return [
            pltpu.make_async_copy(
                new_ref.at[:, 8 * i : 8 * i + 8, z], out_ref.at[:, z, first : first + 8], sem.at[i, z]
            )
            for z in range(8)
        ]

    fetch.wait()
    g0 = radial(ghosts(0), ghosts(1), rows(0), rows(1))
    g1 = radial(ghosts(1), rows(0), rows(1), rows(2))
    for f in range(FIELDS):
        new_ref[f, 0] = edge_ref[f, 0] + scale * (g0[f] - g1[f])
        new_ref[f, 1] = edge_ref[f, 1] + scale * g1[f]
    copies = send(0)
    for copy in copies:
        copy.start()
    g0 = radial(rows(nx - 3), rows(nx - 2), rows(nx - 1), ghosts(2))
    g1 = radial(rows(nx - 2), rows(nx - 1), ghosts(2), ghosts(3))
    for f in range(FIELDS):
        new_ref[f, 14] = edge_ref[f, 14] - scale * g0[f]
        new_ref[f, 15] = edge_ref[f, 15] + scale * (g0[f] - g1[f])
    more = send(1)
    for copy in more:
        copy.start()
    for copy in copies + more:
        copy.wait()


def swaps(nx, ny):
    def at(g, j):
        return (g % nx) * ny + j % ny

    grid = [(g, j) for g in range(nx) for j in range(ny)]
    core = [(at(g, j), at(g, j ^ 1)) for g, j in grid]
    cross = [(at(g, j), at(g, j + 1 if j % 2 else j - 1)) for g, j in grid]
    along = [(at(g, j), at(g ^ 1, j)) for g, j in grid]

    def ends(k):
        there = [(at(0, j), at(nx - 1, j + k)) for j in range(ny)]
        return there + [(b, a) for a, b in there]

    def other(k):
        inside = [(at(g, j), at(g + 1 if g % 2 else g - 1, j)) for g, j in grid if 0 < g < nx - 1]
        return inside + ends(k)

    return core, cross, along, other


def on_device(old_state, section_prims, shear_whole, shear_frac):
    n_gx, n_gy = lax.axis_size("gx"), lax.axis_size("gy")
    gx, gy = lax.axis_index("gx"), lax.axis_index("gy")
    fields, nz, nx, cells = section_prims.shape
    assert (fields, nz, cells) == (FIELDS, 8, 128)
    assert nx % (2 * ROWS) == 0 and n_gx % 2 == 0 and n_gy % 2 == 0
    axes = ("gx", "gy")
    core, cross, along, other = swaps(n_gx, n_gy)
    f32 = jnp.float32
    vmem = pl.BlockSpec(memory_space=pltpu.VMEM)
    smem = pl.BlockSpec(memory_space=pltpu.SMEM)
    hbm = pl.BlockSpec(memory_space=pltpu.HBM)
    block = (fields, nx, nz, cells)
    tile = (fields, nz, cells)
    tiles = nx // ROWS
    edge_rows = jax.ShapeDtypeStruct((fields, 2, nz, cells), f32)

    def room(mib):
        return pltpu.CompilerParams(vmem_limit_bytes=mib << 20)

    def cost(flops):
        n = nx * nz * cells
        return pl.CostEstimate(flops=flops * n, bytes_accessed=12 * fields * n, transcendentals=0)

    w, old = (pltpu.with_memory_space_constraint(v, pltpu.HBM) for v in (section_prims, old_state))
    wt, xa, own, ex, acc = pl.pallas_call(
        functools.partial(pack_kernel, nx),
        out_shape=(
            jax.ShapeDtypeStruct(block, f32),
            edge_rows,
            jax.ShapeDtypeStruct((fields, tiles, nz, cells), f32),
            jax.ShapeDtypeStruct((fields, 2 + tiles // 2, nz, cells), f32),
            jax.ShapeDtypeStruct(block, f32),
        ),
        in_specs=[hbm],
        out_specs=(vmem,) * 5,
        scratch_shapes=[pltpu.SemaphoreType.DMA((2, nz))],
        compiler_params=room(8),
        name="pack",
    )(w)

    c_in = lax.ppermute(ex, axes, core)
    y_in = lax.ppermute(ex, axes, cross)
    xa_in = lax.ppermute(xa, axes, along)
    acc = pl.pallas_call(
        functools.partial(upright_kernel, nx),
        out_shape=jax.ShapeDtypeStruct(block, f32),
        in_specs=[vmem, vmem],
        out_specs=vmem,
        input_output_aliases={1: 0},
        compiler_params=room(8),
        cost_estimate=cost(300),
        name="upright",
    )(wt, acc)
    xb = pl.pallas_call(
        shear_kernel,
        out_shape=edge_rows,
        in_specs=[smem, smem, vmem, vmem, vmem, pl.BlockSpec(memory_space=pl.ANY)],
        out_specs=vmem,
        compiler_params=room(8),
        name="shear",
    )(shear_whole, shear_frac, ex, c_in, y_in, acc)

    def branch(k):
        def run(xb, wt, acc, old, own, c_in, y_in):
            xb_in = lax.ppermute(xb, axes, other(k))
            out, edge = pl.pallas_call(
                functools.partial(inner_kernel, nx),
                out_shape=(
                    jax.ShapeDtypeStruct(section_prims.shape, f32),
                    jax.ShapeDtypeStruct((fields, 16, nz, cells), f32),
                ),
                in_specs=[vmem, vmem, hbm, vmem, vmem, vmem],
                out_specs=(hbm, vmem),
                scratch_shapes=[pltpu.VMEM(block, f32)] * 2
                + [pltpu.VMEM((fields, nx - 16, nz, cells), f32)]
                + [pltpu.VMEM((fields, tiles, nz, cells), f32)]
                + [pltpu.VMEM(tile, f32)] * 3
                + [pltpu.VMEM(block, f32)] * 4
                + [pltpu.SemaphoreType.DMA((1, nz)), pltpu.SemaphoreType.DMA((2, nz))],
                compiler_params=room(16),
                cost_estimate=cost(480),
                name="inner",
            )(wt, acc, old, own, c_in, y_in)
            return xb_in, out, edge

        return run

    whole = lax.shift_right_logical(shear_whole[0], 7)
    xb_in, out, edge = lax.switch(
        whole, [branch(k) for k in range(n_gy)], xb, wt, acc, old, own, c_in, y_in
    )
    return pl.pallas_call(
        functools.partial(outer_kernel, nx),
        out_shape=jax.ShapeDtypeStruct(section_prims.shape, f32),
        in_specs=[vmem] * 3 + [hbm, hbm],
        out_specs=hbm,
        input_output_aliases={4: 0},
        scratch_shapes=[
            pltpu.VMEM((fields, 16, nz, cells), f32),
            pltpu.VMEM((fields, 2, nz, cells), f32),
            pltpu.SemaphoreType.DMA((2, nz)),
            pltpu.SemaphoreType.DMA,
        ],
        compiler_params=room(8),
        name="outer",
    )(wt, edge, xa_in, xb_in, out)


def solution(mesh):
    in_specs = (P(None, None, "gx", "gy"), P(None, None, "gx", "gy"), P(), P())
    out_specs = P(None, None, "gx", "gy")
    return jax.shard_map(
        on_device, mesh=mesh, in_specs=in_specs, out_specs=out_specs, check_vma=False
    )
```

```python
import functools

import jax
import jax.numpy as jnp
from jax import lax
from jax.experimental import pallas as pl
from jax.experimental.pallas import tpu as pltpu
from jax.sharding import PartitionSpec as P

gamma_gas = 5.0 / 3.0
omega_rate = 1.0
shear_rate = 1.5
time_step = 0.1

FIELDS = 8
EDGE = 8
ROWS = 128 // EDGE


def median0(a, b):
    return jnp.maximum(jnp.minimum(a, b), jnp.minimum(jnp.maximum(a, b), 0.0))


def half_slope(a, b):
    return 0.5 * median0(a, b)


def side(w, n):
    t, u = (n + 1) % 3, (n + 2) % 3
    rho, p = w[0], w[4]
    vn, vt, vu = w[1 + n], w[1 + t], w[1 + u]
    bn, bt, bu = w[5 + n], w[5 + t], w[5 + u]
    mn, mt, mu = rho * vn, rho * vt, rho * vu
    mnvn = mn * vn
    bn2 = bn * bn
    bt2 = bt * bt + bu * bu
    bsq = bn2 + bt2
    q = 0.5 * (mnvn + mt * vt + mu * vu) + p * (1.0 / (gamma_gas - 1.0))
    pm = 0.5 * bsq
    cons = [None] * FIELDS
    flux = [None] * FIELDS
    cons[0], cons[1 + n], cons[1 + t], cons[1 + u] = rho, mn, mt, mu
    cons[4] = q + pm
    cons[5 + n], cons[5 + t], cons[5 + u] = bn, bt, bu
    flux[0] = mn
    flux[1 + n] = mnvn + (p + pm - bn2)
    flux[1 + t] = mt * vn - bt * bn
    flux[1 + u] = mu * vn - bu * bn
    flux[4] = (q + p + bt2) * vn - bn * (vt * bt + vu * bu)
    flux[5 + t] = bt * vn - vt * bn
    flux[5 + u] = bu * vn - vu * bn
    a = (0.5 * gamma_gas) * p
    diff = a - pm
    disc = diff * diff + a * (bt2 + bt2)
    x = a + pm + disc * lax.rsqrt(jnp.maximum(disc, 1e-30))
    speed = jnp.abs(vn) + x * lax.rsqrt(rho * x)
    return cons, flux, speed


def twice_face(left, right, n):
    cl, fl, sl = side(left, n)
    cr, fr, sr = side(right, n)
    s = jnp.maximum(sl, sr)
    out = []
    for j in range(FIELDS):
        jump = s * (cr[j] - cl[j])
        out.append(-jump if j == 5 + n else fl[j] + fr[j] - jump)
    return out


def lanes():
    return lax.broadcasted_iota(jnp.int32, (8, 128), 1)


def rows_of(ref, x):
    return [ref[f, x] for f in range(FIELDS)]


def transposing(src, dst, sem, parts):
    n = FIELDS // parts
    return [
        [
            pltpu.make_async_copy(
                src.at[n * i : n * i + n, z], dst.at[n * i : n * i + n, :, z], sem.at[i, z]
            )
            for z in range(8)
        ]
        for i in range(parts)
    ]


def upright(nx, wt_ref, acc_ref):
    def body(x, _):
        w = rows_of(wt_ref, x)
        left, right = [], []
        for f in range(FIELDS):
            up = pltpu.roll(w[f], 7, 0) - w[f]
            h = half_slope(pltpu.roll(up, 1, 0), up)
            left.append(w[f] + h)
            right.append(pltpu.roll(w[f] - h, 7, 0))
        g = twice_face(left, right, 2)
        rho, vx, vy, vz, p, bx, by, bz = w
        mx, my, mz = rho * vx, rho * vy, rho * vz
        energy = (
            p * (1.0 / (gamma_gas - 1.0))
            + 0.5 * (mx * vx + my * vy + mz * vz)
            + 0.5 * (bx * bx + by * by + bz * bz)
        )
        cons = [rho, mx, my, mz, energy, bx, by, bz]
        src = [None] * FIELDS
        src[1] = (time_step * 2.0 * omega_rate) * my
        src[2] = (-time_step * (2.0 - shear_rate) * omega_rate) * mx
        src[4] = (time_step * shear_rate * omega_rate) * (mx * vy - bx * by)
        src[6] = (-time_step * shear_rate * omega_rate) * bx
        for f in range(FIELDS):
            total = cons[f] + (0.5 * time_step) * (pltpu.roll(g[f], 1, 0) - g[f])
            acc_ref[f, x] = total if src[f] is None else total + src[f]
        return 0

    lax.fori_loop(0, nx, body, 0)


def radial_open(wt_ref, l_ref, d_ref, g_ref):
    for f in range(FIELDS):
        g_ref[f] = jnp.zeros((8, 128), jnp.float32)
        l_ref[f] = wt_ref[f, 0]
        d_ref[f] = wt_ref[f, 1] - wt_ref[f, 0]


def radial_rows(nx, rows, wt_ref, l_ref, d_ref, g_ref):
    l, d, below = ([ref[f] for f in range(FIELDS)] for ref in (l_ref, d_ref, g_ref))
    out = []
    for x in rows:
        w2 = rows_of(wt_ref, jnp.minimum(x + 1, nx - 1))
        w3 = rows_of(wt_ref, jnp.minimum(x + 2, nx - 1))
        right, next_l, next_d = [], [], []
        for f in range(FIELDS):
            step = w3[f] - w2[f]
            h = half_slope(d[f], step)
            right.append(w2[f] - h)
            next_l.append(w2[f] + h)
            next_d.append(step)
        keep = jnp.where((x > 0) & (x < nx - 2), 1.0, 0.0)
        g = [keep * v for v in twice_face(l, right, 0)]
        out.append([below[f] - g[f] for f in range(FIELDS)])
        l, d, below = next_l, next_d, g
    for f in range(FIELDS):
        l_ref[f], d_ref[f], g_ref[f] = l[f], d[f], below[f]
    return out


def radial_sweep(nx, wt_ref, acc_ref, *carry):
    radial_open(wt_ref, *carry)

    def body(i, _):
        rows = (i * 2, i * 2 + 1)
        for x, div in zip(rows, radial_rows(nx, rows, wt_ref, *carry)):
            for f in range(FIELDS):
                acc_ref[f, x] = acc_ref[f, x] + (0.5 * time_step) * div[f]
        return 0

    lax.fori_loop(0, nx // 2, body, 0)


def early():
    return (lax.axis_index("gx") == 0) & (lax.axis_index("gy") < 2)


def ahead():
    return early() | (lax.axis_index("gx") == 1)


def upright_kernel(nx, wt_ref, acc_in, acc_ref, *carry):
    @pl.when(jnp.logical_not(early()))
    def _():
        upright(nx, wt_ref, acc_ref)

    @pl.when(ahead())
    def _():
        radial_sweep(nx, wt_ref, acc_ref, *carry)


def pack_kernel(nx, w_ref, wt_ref, xa_ref, own_ref, ex_ref, acc_ref, sem):
    parts = sem.shape[0]
    copies = transposing(w_ref, wt_ref, sem, parts)
    for part in copies:
        for copy in part:
            copy.start()
    odd = lax.rem(lax.axis_index("gx"), 2)
    first_a = (1 - odd) * (nx - 2)
    first_b = odd * (nx - 2)
    lane = lanes()
    group, place = lane // EDGE, lax.rem(lane, EDGE)
    middle = (place > 1) & (place < 6)
    for f in range(FIELDS):
        if f % (FIELDS // parts) == 0:
            for copy in copies[f // (FIELDS // parts)]:
                copy.wait()
        for g in range(2):
            xa_ref[f, g] = wt_ref[f, first_a + g]
            ex_ref[f, g] = wt_ref[f, first_b + g]
        tiles = []
        for v in range(nx // ROWS):
            acc = jnp.zeros((8, 128), jnp.float32)
            for i in range(ROWS):
                row = wt_ref[f, v * ROWS + i]
                acc = jnp.where(group == i, pltpu.roll(row, (EDGE * i + 4) % 128, 1), acc)
            own_ref[f, v] = acc
            tiles.append(acc)
        for v in range(0, len(tiles), 2):
            ex_ref[f, 2 + v // 2] = jnp.where(middle, tiles[v], pltpu.roll(tiles[v + 1], 4, 1))

    @pl.when(early())
    def _():
        upright(nx, wt_ref, acc_ref)


def shear_kernel(whole_ref, frac_ref, ex_ref, c_ref, y_ref, acc_ref, xb_ref):
    gx, odd_y = lax.axis_index("gx"), lax.rem(lax.axis_index("gy"), 2)
    upper = gx == lax.axis_size("gx") - 1
    end = upper | (gx == 0)
    shift = jnp.where(end, lax.rem(whole_ref[0], 128), 0)
    frac = jnp.where(end, frac_ref[0], 0.0)
    sibling = (odd_y == 1) != upper
    lane = lanes()

    def window(own, other, s):
        amount = jnp.where(upper, lax.rem(128 - s, 128), lax.rem(s, 128))
        low = jnp.where(upper, 0, s)
        high = jnp.where(upper, 128 - s, 128)
        near = (lane >= low) & (lane < high)
        return pltpu.roll(own, amount, 1), pltpu.roll(other, amount, 1), near

    for f in range(FIELDS):
        for g in range(2):
            own = ex_ref[f, g]
            other = jnp.where(sibling, c_ref[f, g], y_ref[f, g])
            a, b, near = window(own, other, shift)
            first = jnp.where(near, a, b)
            a, b, near = window(own, other, shift + 1)
            second = jnp.where(near, a, b)
            xb_ref[f, g] = (1.0 - frac) * first + frac * second


def inner_kernel(
    nx, wt_ref, up_ref, old_ref, own_ref, c_ref, y_ref, out_ref, edge_ref,
    acc_ref, old_t, new_ref, q_ref, g_ref, l_ref, d_ref, al_ref, am_ref, ar_ref, ag_ref, sem, out_sem,
):
    copies = transposing(old_ref, old_t, sem, 1)[0]
    for copy in copies:
        copy.start()
    lane = lanes()
    whole = (lane > 0) & (lane < 126)

    def states(x):
        for f in range(FIELDS):
            w = wt_ref[f, x]
            h = half_slope(w - pltpu.roll(w, 1, 1), pltpu.roll(w, 127, 1) - w)
            al_ref[f, x] = w + h
            am_ref[f, x] = w - h

    def turn(x):
        for f in range(FIELDS):
            ar_ref[f, x] = pltpu.roll(am_ref[f, x], 127, 1)

    def faces(x):
        g = twice_face(rows_of(al_ref, x), rows_of(ar_ref, x), 1)
        for f in range(FIELDS):
            ag_ref[f, x] = jnp.where(whole, g[f], 0.0)

    def sweep(step, radial):
        for i in range(3 * step):
            states(i)
        for i in range(2 * step):
            turn(i)
        for i in range(step):
            faces(i)
        carry = (l_ref, d_ref, g_ref)
        if radial:
            radial_open(wt_ref, *carry)

        def body(i, _):
            rows = [i * step + j for j in range(step)]
            divs = [[pltpu.roll(v, 1, 1) - v for v in rows_of(ag_ref, x)] for x in rows]
            for stage, reach in ((faces, 1), (turn, 2), (states, 3)):
                for x in rows:
                    stage(jnp.minimum(x + reach * step, nx - 1))
            if radial:
                more = radial_rows(nx, rows, wt_ref, *carry)
                divs = [[a + b for a, b in zip(*pair)] for pair in zip(divs, more)]
            for x, div in zip(rows, divs):
                for f in range(FIELDS):
                    acc_ref[f, x] = up_ref[f, x] + (0.5 * time_step) * div[f]
            return 0

        lax.fori_loop(0, nx // step, body, 0)

    @pl.when(ahead())
    def _():
        sweep(4, False)

    @pl.when(jnp.logical_not(ahead()))
    def _():
        sweep(2, True)

    odd_y = lax.rem(lax.axis_index("gy"), 2)
    scale = 0.25 * time_step
    place = lax.rem(lane, EDGE)
    low = place < 4
    for v in range(nx // ROWS):
        left, right = [], []
        for f in range(FIELDS):
            own, core, cross = own_ref[f, v], c_ref[f, 2 + v // 2], y_ref[f, 2 + v // 2]
            before = jnp.where(odd_y == 1, core, cross)
            after = jnp.where(odd_y == 1, cross, core)
            if v % 2:
                before, after = pltpu.roll(before, 124, 1), pltpu.roll(after, 124, 1)
            end = jnp.where(low, own, after)
            start = jnp.where(low, before, own)
            w0 = jnp.where(low, pltpu.roll(end, 1, 1), pltpu.roll(start, 2, 1))
            w1 = jnp.where(low, end, pltpu.roll(start, 1, 1))
            w2 = jnp.where(low, pltpu.roll(end, 127, 1), start)
            w3 = jnp.where(low, pltpu.roll(end, 126, 1), pltpu.roll(start, 127, 1))
            mid = w2 - w1
            left.append(w1 + half_slope(w1 - w0, mid))
            right.append(w2 - half_slope(mid, w3 - w2))
        g = twice_face(left, right, 1)
        for f in range(FIELDS):
            lower = jnp.where(low, jnp.where(place == 3, pltpu.roll(g[f], 1, 1), 0.0), g[f])
            upper = jnp.where(low, g[f], jnp.where(place == 4, pltpu.roll(g[f], 127, 1), 0.0))
            q_ref[f, v] = scale * (lower - upper)

    for copy in copies:
        copy.wait()
    ends = (lane < 2) | (lane > 125)
    parts = out_sem.shape[0]
    copies = []
    for f in range(FIELDS):
        for x in range(nx):
            q = pltpu.roll(q_ref[f, x // ROWS], (124 - EDGE * (x % ROWS)) % 128, 1)
            new = 0.5 * (acc_ref[f, x] + old_t[f, x]) + jnp.where(ends, q, 0.0)
            if x < 8:
                edge_ref[f, x] = new
            elif x >= nx - 8:
                edge_ref[f, x - nx + 16] = new
            else:
                new_ref[f, x - 8] = new
        if (f + 1) % (FIELDS // parts) == 0:
            part = (f + 1) // (FIELDS // parts) - 1
            span = slice(f + 1 - FIELDS // parts, f + 1)
            for z in range(8):
                copy = pltpu.make_async_copy(
                    new_ref.at[span, :, z], out_ref.at[span, z, 8 : nx - 8], out_sem.at[part, z]
                )
                copy.start()
                copies.append(copy)
    for copy in copies:
        copy.wait()


def outer_kernel(
    nx, wt_ref, edge_ref, xa_ref, xb_ref, part_ref, out_ref, new_ref, sem
):
    odd_x = lax.rem(lax.axis_index("gx"), 2)
    scale = 0.25 * time_step
    for f in range(FIELDS):
        for i in range(16):
            new_ref[f, i] = edge_ref[f, i]

    def rows(x):
        return rows_of(wt_ref, x)

    def ghosts(i):
        above = (odd_x == 1) != (i < 2)
        return [jnp.where(above, xb_ref[f, i % 2], xa_ref[f, i % 2]) for f in range(FIELDS)]

    def radial(w0, w1, w2, w3):
        left, right = [], []
        for f in range(FIELDS):
            mid = w2[f] - w1[f]
            left.append(w1[f] + half_slope(w1[f] - w0[f], mid))
            right.append(w2[f] - half_slope(mid, w3[f] - w2[f]))
        return twice_face(left, right, 0)

    def send(i):
        first = (nx - 8) * i
        return [
            pltpu.make_async_copy(
                new_ref.at[:, 8 * i : 8 * i + 8, z], out_ref.at[:, z, first : first + 8], sem.at[i, z]
            )
            for z in range(8)
        ]

    g0 = radial(ghosts(0), ghosts(1), rows(0), rows(1))
    g1 = radial(ghosts(1), rows(0), rows(1), rows(2))
    for f in range(FIELDS):
        new_ref[f, 0] = edge_ref[f, 0] + scale * (g0[f] - g1[f])
        new_ref[f, 1] = edge_ref[f, 1] + scale * g1[f]
    copies = send(0)
    for copy in copies:
        copy.start()
    g0 = radial(rows(nx - 3), rows(nx - 2), rows(nx - 1), ghosts(2))
    g1 = radial(rows(nx - 2), rows(nx - 1), ghosts(2), ghosts(3))
    for f in range(FIELDS):
        new_ref[f, 14] = edge_ref[f, 14] - scale * g0[f]
        new_ref[f, 15] = edge_ref[f, 15] + scale * (g0[f] - g1[f])
    more = send(1)
    for copy in more:
        copy.start()
    for copy in copies + more:
        copy.wait()


def swaps(nx, ny):
    def at(g, j):
        return (g % nx) * ny + j % ny

    grid = [(g, j) for g in range(nx) for j in range(ny)]
    core = [(at(g, j), at(g, j ^ 1)) for g, j in grid]
    cross = [(at(g, j), at(g, j + 1 if j % 2 else j - 1)) for g, j in grid]
    along = [(at(g, j), at(g ^ 1, j)) for g, j in grid]

    def ends(k):
        there = [(at(0, j), at(nx - 1, j + k)) for j in range(ny)]
        return there + [(b, a) for a, b in there]

    def other(k):
        inside = [(at(g, j), at(g + 1 if g % 2 else g - 1, j)) for g, j in grid if 0 < g < nx - 1]
        return inside + ends(k)

    return core, cross, along, other


def on_device(old_state, section_prims, shear_whole, shear_frac):
    n_gx, n_gy = lax.axis_size("gx"), lax.axis_size("gy")
    gx, gy = lax.axis_index("gx"), lax.axis_index("gy")
    fields, nz, nx, cells = section_prims.shape
    assert (fields, nz, cells) == (FIELDS, 8, 128)
    assert nx % (2 * ROWS) == 0 and nx >= 32 and n_gx % 2 == 0 and n_gy % 2 == 0
    axes = ("gx", "gy")
    core, cross, along, other = swaps(n_gx, n_gy)
    f32 = jnp.float32
    vmem = pl.BlockSpec(memory_space=pltpu.VMEM)
    smem = pl.BlockSpec(memory_space=pltpu.SMEM)
    hbm = pl.BlockSpec(memory_space=pltpu.HBM)
    block = (fields, nx, nz, cells)
    tile = (fields, nz, cells)
    tiles = nx // ROWS
    edge_rows = jax.ShapeDtypeStruct((fields, 2, nz, cells), f32)

    def room(mib):
        return pltpu.CompilerParams(vmem_limit_bytes=mib << 20)

    def cost(flops):
        n = nx * nz * cells
        return pl.CostEstimate(flops=flops * n, bytes_accessed=12 * fields * n, transcendentals=0)

    w, old = (pltpu.with_memory_space_constraint(v, pltpu.HBM) for v in (section_prims, old_state))
    wt, xa, own, ex, acc = pl.pallas_call(
        functools.partial(pack_kernel, nx),
        out_shape=(
            jax.ShapeDtypeStruct(block, f32),
            edge_rows,
            jax.ShapeDtypeStruct((fields, tiles, nz, cells), f32),
            jax.ShapeDtypeStruct((fields, 2 + tiles // 2, nz, cells), f32),
            jax.ShapeDtypeStruct(block, f32),
        ),
        in_specs=[hbm],
        out_specs=(vmem,) * 5,
        scratch_shapes=[pltpu.SemaphoreType.DMA((2, nz))],
        compiler_params=room(8),
        name="pack",
    )(w)

    c_in = lax.ppermute(ex, axes, core)
    y_in = lax.ppermute(ex, axes, cross)
    xa_in = lax.ppermute(xa, axes, along)
    acc = pl.pallas_call(
        functools.partial(upright_kernel, nx),
        out_shape=jax.ShapeDtypeStruct(block, f32),
        in_specs=[vmem, vmem],
        out_specs=vmem,
        input_output_aliases={1: 0},
        scratch_shapes=[pltpu.VMEM(tile, f32)] * 3,
        compiler_params=room(8),
        cost_estimate=cost(300),
        name="upright",
    )(wt, acc)
    xb = pl.pallas_call(
        shear_kernel,
        out_shape=edge_rows,
        in_specs=[smem, smem, vmem, vmem, vmem, pl.BlockSpec(memory_space=pl.ANY)],
        out_specs=vmem,
        compiler_params=room(8),
        name="shear",
    )(shear_whole, shear_frac, ex, c_in, y_in, acc)

    def branch(k):
        def run(xb, wt, acc, old, own, c_in, y_in, xa_in):
            xb_in = lax.ppermute(xb, axes, other(k))
            out, edge = pl.pallas_call(
                functools.partial(inner_kernel, nx),
                out_shape=(
                    jax.ShapeDtypeStruct(section_prims.shape, f32),
                    jax.ShapeDtypeStruct((fields, 16, nz, cells), f32),
                ),
                in_specs=[vmem, vmem, hbm, vmem, vmem, vmem],
                out_specs=(hbm, vmem),
                scratch_shapes=[pltpu.VMEM(block, f32)] * 2
                + [pltpu.VMEM((fields, nx - 16, nz, cells), f32)]
                + [pltpu.VMEM((fields, tiles, nz, cells), f32)]
                + [pltpu.VMEM(tile, f32)] * 3
                + [pltpu.VMEM(block, f32)] * 4
                + [pltpu.SemaphoreType.DMA((1, nz)), pltpu.SemaphoreType.DMA((2, nz))],
                compiler_params=room(16),
                cost_estimate=cost(480),
                name="inner",
            )(wt, acc, old, own, c_in, y_in)
            return pl.pallas_call(
                functools.partial(outer_kernel, nx),
                out_shape=jax.ShapeDtypeStruct(section_prims.shape, f32),
                in_specs=[vmem] * 4 + [hbm],
                out_specs=hbm,
                input_output_aliases={4: 0},
                scratch_shapes=[
                    pltpu.VMEM((fields, 16, nz, cells), f32),
                    pltpu.SemaphoreType.DMA((2, nz)),
                ],
                compiler_params=room(8),
                name="outer",
            )(wt, edge, xa_in, xb_in, out)

        return run

    whole = lax.shift_right_logical(shear_whole[0], 7)
    operands = (xb, wt, acc, old, own, c_in, y_in, xa_in)
    return lax.switch(whole, [branch(k) for k in range(n_gy)], *operands)


def solution(mesh):
    in_specs = (P(None, None, "gx", "gy"), P(None, None, "gx", "gy"), P(), P())
    out_specs = P(None, None, "gx", "gy")
    return jax.shard_map(
        on_device, mesh=mesh, in_specs=in_specs, out_specs=out_specs, check_vma=False
    )
```
